32 devices in a mesh: row: 4 (over z), col: 8 (over y, x, core).
Axes of the slice: x: 2, y: 2, z: 4, core: 2. Of those that a mesh axis runs over, the one named last changes fastest.
Arguments:
- density_tiles: bfloat16 [1024, 128, 128], P(('row', 'col')), may hold values from -1 to 1
- send_list: int32 [32, 32, 3], P(('row', 'col')), may hold values from 0 to 31
- basis_values: bfloat16 [64, 2048, 768], P(('row', 'col')), may hold values from -0.625 to 0.625
- active_blocks: int32 [64], P(('row', 'col')), may hold values from 1 to 6, as said below
- touch_slots: int32 [64, 6, 6], P(('row', 'col')), may hold values from -1 to 95, as said below
- point_weights: float32 [64, 2048], P(('row', 'col')), may hold values from 0.2 to 2
- harmonics: float32 [64, 49, 2048], P(('row', 'col')), may hold values from -1.2 to 1.2
- shell_index: int32 [64, 2048], P(('row', 'col')), may hold values from 0 to 127
- batch_atom: int32 [64], P(('row', 'col')), may hold values from 0 to 15
- radial_green: float32 [7, 128, 128], replicated, may hold values from -0.25 to 0.25
Outputs:
- ham_tiles: float32 [1024, 128, 128], P(('row', 'col'))
- multipoles: float32 [16, 49, 128], P('col')
The draws below stay inside these ranges and needn't reach their ends.
Inputs may be any that keep to these rules, and one draw needn't show every extreme that they name: `active_blocks`: every batch has 1 to 6 active blocks; some batch has 6. `touch_slots`: -1 exactly at pairs with a block at or beyond the batch's active count; the other entries are distinct among the batches of one device, and a slot s names source device s // 3 along row+col.
All inputs are finite; a program needn't handle non-finite values.
Results may differ from the reference program's by a relative error of at most 0.0029.
Values may be sent and summed in bfloat16 or wider, within the bound.
No kernel may reach another device: no remote copies, remote signals or barrier semaphores. Data moves between devices by JAX's collectives and lax.ppermute only.
A program may use at most 128 MiB of HBM per device.

```python
import math
import jax
import jax.numpy as jnp
from jax import lax

BLK = 128
NA = 6
PTS = 2048
SHELLS = 128
LDEG = 7
BATCH_DEV = 2
TILES_DEV = 32
HARM = 49
NATOM = 16
NBATCH = 64
NTILE = 1024
CAP = 3
DEVICES = 32


def plan_slots(key):
    groups = NBATCH // BATCH_DEV
    counts = jax.random.randint(jax.random.fold_in(key, 11), (NBATCH,), max(1, NA - 2), NA + 1)
    counts = counts.at[0].set(NA)
    places = jnp.arange(NA)
    live_pairs = (places[None, :, None] < counts[:, None, None]) & (places[None, None, :] < counts[:, None, None])
    live_pairs = live_pairs.reshape(groups, BATCH_DEV * NA * NA).astype(jnp.int32)
    rank_order = jnp.cumsum(live_pairs, axis=1) - 1
    shuffles = jax.vmap(lambda sub_key: jax.random.permutation(sub_key, groups))(jax.random.split(jax.random.fold_in(key, 12), groups))
    source = jnp.take_along_axis(shuffles, jnp.maximum(rank_order, 0) % groups, axis=1)
    slot_ids = source * CAP + jnp.maximum(rank_order, 0) // groups
    slot_ids = jnp.where(live_pairs > 0, slot_ids, -1).reshape(NBATCH, NA, NA)
    return (counts.astype(jnp.int32), slot_ids.astype(jnp.int32))


def draw_active_blocks(key, part):
    return plan_slots(key)[0]


def draw_touch_slots(key, part):
    return plan_slots(key)[1]


def with_ends(drawn, key, least, high):
    spot = [jax.random.randint(jax.random.fold_in(key, axis), (), 0, length) for axis, length in enumerate(drawn.shape)]
    longest = drawn.shape.index(max(drawn.shape))
    neighbour = spot[:longest] + [(spot[longest] + 1) % drawn.shape[longest]] + spot[longest + 1:]
    return drawn.at[tuple(spot)].set(least).at[tuple(neighbour)].set(high)


def shard_levels(stream_key, dims, cuts, low, largest):
    factor_of, own = 1.0, jax.random.fold_in(stream_key, 6)
    for dim, parts in cuts:
        draws = jnp.exp(jax.random.uniform(jax.random.fold_in(own, dim), (parts,), jnp.float32, low / len(cuts), largest / len(cuts)))
        factor_of = factor_of * jnp.repeat(draws, dims[dim] // parts).reshape([-1 if axis == dim else 1 for axis in range(len(dims))])
    return factor_of


def noise(stream_key, extent, scale, reach, cuts=(), held_as=jnp.bfloat16):
    result = jax.random.normal(stream_key, extent, jnp.float32) * scale
    if len(cuts) > 0:
        result = shard_levels(stream_key, extent, cuts, -0.22, 0.18) * result
    return jnp.clip(result, min=-reach, max=reach).astype(held_as)


def setup_inputs(seed: int = 0) -> dict:
    streams_of = jax.random.split(jax.random.key(seed), 11)
    return {
        "density_tiles": noise(streams_of[0], (NTILE, BLK, BLK), 0.125, 1.0, ((0, 32),)),
        "send_list": with_ends(jax.random.randint(streams_of[1], (DEVICES, DEVICES, CAP), 0, TILES_DEV), jax.random.fold_in(streams_of[1], 1), 0, TILES_DEV - 1).astype(jnp.int32),
        "basis_values": noise(streams_of[2], (NBATCH, PTS, NA * BLK), (NA * BLK // 8) ** -0.5, 0.625, ((0, 32),)),
        "active_blocks": draw_active_blocks(jax.random.fold_in(streams_of[10], 71), 0),
        "touch_slots": draw_touch_slots(jax.random.fold_in(streams_of[10], 71), 0),
        "point_weights": jnp.clip(jnp.exp(math.log(2.0) - 2.3025851 * jax.random.uniform(streams_of[5], (NBATCH, PTS), jnp.float32) ** shard_levels(streams_of[5], (NBATCH, PTS), ((0, 32),), -0.2, 0.2)), 0.2, 2.0),
        "harmonics": noise(streams_of[6], (NBATCH, HARM, PTS), 0.2, 1.2, ((0, 32),), jnp.float32),
        "shell_index": with_ends(jax.random.randint(streams_of[7], (NBATCH, PTS), 0, SHELLS), jax.random.fold_in(streams_of[7], 1), 0, SHELLS - 1).astype(jnp.int32),
        "batch_atom": with_ends(jax.random.randint(streams_of[8], (NBATCH,), 0, NATOM), jax.random.fold_in(streams_of[8], 1), 0, NATOM - 1).astype(jnp.int32),
        "radial_green": noise(streams_of[9], (LDEG, SHELLS, SHELLS), (4 * SHELLS) ** -0.5, 0.25, (), jnp.float32),
    }


def degrees(harm_count):
    harm_ids = jnp.arange(harm_count)
    bounds = jnp.arange(1, LDEG) ** 2
    return jnp.sum((harm_ids[:, None] >= bounds[None, :]).astype(jnp.int32), axis=1)


def shells_table(shell_row):
    return (shell_row[:, None] == jnp.arange(SHELLS)[None, :]).astype(jnp.float32)


def prepare(batch, density_tiles, send_list, basis_values, active_blocks, touch_slots):
    groups = NBATCH // BATCH_DEV
    span_width = NA * BLK
    home_dev = batch // BATCH_DEV
    active = active_blocks[batch]
    places = jnp.arange(NA)
    pair_mask = (places[:, None] < active) & (places[None, :] < active)
    slot_ids = jnp.clip(touch_slots[batch], 0, groups * CAP - 1)
    source = slot_ids // CAP
    local_ids = send_list[source, home_dev, slot_ids % CAP]
    tile_ids = (source * TILES_DEV + local_ids).astype(jnp.int32)
    tile_set = density_tiles[tile_ids]
    tile_set = jnp.where(pair_mask[:, :, None, None], tile_set, jnp.zeros_like(tile_set))
    matrix = jnp.transpose(tile_set, (0, 2, 1, 3)).reshape(span_width, span_width)
    column = jnp.arange(span_width) // BLK < active
    values = jnp.where(column[None, :], basis_values[batch], jnp.zeros_like(basis_values[batch]))
    return values, matrix, tile_ids, pair_mask


def reference(density_tiles, send_list, basis_values, active_blocks, touch_slots, point_weights, harmonics, shell_index, batch_atom, radial_green):
    highest = lax.Precision.HIGHEST

    def first_pass(batch):
        values, matrix, tile_ids, pair_mask = prepare(batch, density_tiles, send_list, basis_values, active_blocks, touch_slots)
        product = jnp.dot(values, matrix, preferred_element_type=jnp.float32)
        density = jnp.sum(product * values, axis=1)
        onehot = shells_table(shell_index[batch])
        weighted = harmonics[batch] * (point_weights[batch] * density)[None, :]
        moment = jnp.dot(weighted, onehot, precision=highest)
        return density, moment

    density_all, moment_all = lax.map(first_pass, jnp.arange(NBATCH))
    atom_hot = (batch_atom[:, None] == jnp.arange(NATOM)[None, :]).astype(jnp.float32)
    atom_mom = jnp.einsum("ba,bhs->ahs", atom_hot, moment_all, precision=highest)
    green_h = radial_green[degrees(HARM)]
    multipoles = jnp.einsum("hst,aht->ahs", green_h, atom_mom, precision=highest)

    def add_batch(ham_tiles, batch):
        values, matrix, tile_ids, pair_mask = prepare(batch, density_tiles, send_list, basis_values, active_blocks, touch_slots)
        density = density_all[batch]
        onehot = shells_table(shell_index[batch])
        atom_pot = multipoles[batch_atom[batch]]
        pot_points = jnp.dot(atom_pot, onehot.T, precision=highest)
        hartree = jnp.sum(harmonics[batch] * pot_points, axis=0)
        potential = hartree - density * jnp.power(1.0 + density * density, -1.0 / 3.0)
        scaled = (values * (point_weights[batch] * potential)[:, None]).astype(jnp.bfloat16)
        ham_batch = jnp.dot(values.T, scaled, preferred_element_type=jnp.float32)
        pieces = jnp.transpose(ham_batch.reshape(NA, BLK, NA, BLK), (0, 2, 1, 3))
        pieces = jnp.where(pair_mask[:, :, None, None], pieces, jnp.zeros_like(pieces))
        return ham_tiles.at[tile_ids.reshape(-1)].add(pieces.reshape(NA * NA, BLK, BLK)), None

    start = jnp.zeros((NTILE, BLK, BLK), jnp.float32)
    ham_tiles, _ = lax.scan(add_batch, start, jnp.arange(NBATCH))
    return ham_tiles, multipoles
```

```python
import jax
import jax.numpy as jnp
from jax import lax
from jax.experimental import pallas as pl
from jax.experimental.pallas import tpu as pltpu
from jax.sharding import PartitionSpec as P

LDEG = 7
ATOM_COL = 2
AXES = ("row", "col")
F32 = jnp.float32
BF16 = jnp.bfloat16
NT = (((1,), (1,)), ((), ()))


def degrees(harm_ids):
    bounds = jnp.arange(1, LDEG) ** 2
    return jnp.sum((harm_ids[:, None] >= bounds[None, :]).astype(jnp.int32), axis=1)


def full(shape):
    return pl.BlockSpec(shape, lambda *_: (0,) * len(shape), pipeline_mode=pl.Buffered(1))


def params(mib):
    return pltpu.CompilerParams(
        dimension_semantics=("arbitrary",), vmem_limit_bytes=mib * 1024 * 1024
    )


def split3(values):
    high = values.astype(BF16)
    rest = values - high.astype(F32)
    mid = rest.astype(BF16)
    low = (rest - mid.astype(F32)).astype(BF16)
    return jnp.concatenate([high, mid, low], axis=0)


def join3(stacked):
    rows = stacked.shape[0] // 3
    return stacked[:rows] + (stacked[rows : 2 * rows] + stacked[2 * rows :])


def gather_tiles(tile_ids, tiles):
    count = tile_ids.shape[0]
    _, blk, _ = tiles.shape
    step = count // 8

    def body(ids, tiles_ref, out_ref):
        first = pl.program_id(0) * step
        for place in range(step):
            out_ref[place] = tiles_ref[ids[first + place]]

    return pl.pallas_call(
        body,
        out_shape=jax.ShapeDtypeStruct((count, blk, blk), tiles.dtype),
        grid_spec=pltpu.PrefetchScalarGridSpec(
            num_scalar_prefetch=1,
            grid=(count // step,),
            in_specs=[full(tiles.shape)],
            out_specs=pl.BlockSpec((step, blk, blk), lambda i, ids: (i, 0, 0)),
        ),
        compiler_params=params(16),
        name="gather_tiles",
    )(tile_ids, tiles)


def sum_tiles(tile_ids, arrived, tiles_dev):
    count, blk, _ = arrived.shape
    step = count // 8

    def body(ids, arrived_ref, out_ref):
        @pl.when(pl.program_id(0) == 0)
        def _():
            out_ref[...] = jnp.zeros_like(out_ref)

        first = pl.program_id(0) * step
        for place in range(step):
            tile = ids[first + place]
            out_ref[tile] = out_ref[tile] + arrived_ref[place].astype(F32)

    return pl.pallas_call(
        body,
        out_shape=jax.ShapeDtypeStruct((tiles_dev, blk, blk), F32),
        grid_spec=pltpu.PrefetchScalarGridSpec(
            num_scalar_prefetch=1,
            grid=(count // step,),
            in_specs=[pl.BlockSpec((step, blk, blk), lambda i, ids: (i, 0, 0))],
            out_specs=full((tiles_dev, blk, blk)),
        ),
        compiler_params=params(16),
        name="sum_tiles",
    )(tile_ids, arrived)


def density_pass(active, slots, atoms, received, basis_t, harmonics, weights, shells, share, devices):
    batches, span, points = basis_t.shape
    slot_count, blk, _ = received.shape
    blocks = span // blk
    rows = harmonics.shape[1]
    radial = share[1]
    held = share[0]
    chunk = min(512, points)
    lines = (held + 1) * batches

    def body(act, slot_ids, atom_ids, recv, phi, harm, wts, shell, rho_out, send, matrix, mom_keep):
        batch = pl.program_id(0)
        count = act[batch]

        for i in range(blocks):
            for j in range(blocks):
                spot = (pl.ds(i * blk, blk), pl.ds(j * blk, blk))
                live = (i < count) & (j < count)

                @pl.when(live)
                def _(i=i, j=j, spot=spot):
                    slot = jnp.clip(slot_ids[batch, i * blocks + j], 0, slot_count - 1)
                    matrix[spot] = recv[slot]

                @pl.when(jnp.logical_not(live))
                def _(spot=spot):
                    matrix[spot] = jnp.zeros((blk, blk), BF16)

        def step(at, moments):
            cols = pl.ds(pl.multiple_of(at * chunk, chunk), chunk)
            phi_c = phi[0, :, cols]
            product = jnp.dot(matrix[...], phi_c, preferred_element_type=F32)
            rho = jnp.sum(product * phi_c.astype(F32), axis=0, keepdims=True)
            rho_out[0, :, cols] = rho
            weighted = harm[0, :, cols] * (wts[0, :, cols] * rho)
            ids = lax.broadcasted_iota(jnp.int32, (radial, chunk), 0)
            onehot = jnp.where(shell[0, :, cols] == ids, 1.0, 0.0).astype(BF16)
            return moments + lax.dot_general(
                split3(weighted), onehot, NT, preferred_element_type=F32
            )

        moments = lax.fori_loop(
            0, points // chunk, step, jnp.zeros((3 * rows, radial), F32)
        )
        mom_keep[...] = join3(moments)

        for b in range(batches):

            @pl.when(batch == b)
            def _(b=b):
                for k in range(held):
                    for d in range(devices):
                        line = d * held + k
                        if line < rows:
                            send[d, pl.ds(k * batches + b, 1), :] = mom_keep[pl.ds(line, 1), :]
                        else:
                            send[d, pl.ds(k * batches + b, 1), :] = jnp.zeros((1, radial), F32)
                send[:, pl.ds(held * batches + b, 1), :] = jnp.full(
                    (devices, 1, radial), atom_ids[b].astype(F32), F32
                )

    return pl.pallas_call(
        body,
        out_shape=(
            jax.ShapeDtypeStruct((batches, 1, points), F32),
            jax.ShapeDtypeStruct((devices, lines, radial), F32),
        ),
        grid_spec=pltpu.PrefetchScalarGridSpec(
            num_scalar_prefetch=3,
            grid=(batches,),
            in_specs=[
                full(received.shape),
                pl.BlockSpec((1, span, points), lambda b, *_: (b, 0, 0)),
                pl.BlockSpec((1, rows, points), lambda b, *_: (b, 0, 0)),
                pl.BlockSpec((1, 1, points), lambda b, *_: (b, 0, 0)),
                pl.BlockSpec((1, 1, points), lambda b, *_: (b, 0, 0)),
            ],
            out_specs=(
                pl.BlockSpec((1, 1, points), lambda b, *_: (b, 0, 0)),
                full((devices, lines, radial)),
            ),
            scratch_shapes=[pltpu.VMEM((span, span), BF16), pltpu.VMEM((rows, radial), F32)],
        ),
        compiler_params=params(32),
        name="density_pass",
    )(active, slots, atoms, received, basis_t, harmonics, weights, shells)


def radial_solve(degree_ids, arrived, green, natoms, held, batches, cols_count):
    devices, lines, radial = arrived.shape
    rows_out = (batches + ATOM_COL) * held

    def body(deg, got, green_ref, out, flat):
        for r in range(lines):
            for d in range(devices):
                flat[r, pl.ds(d, 1), :] = got[d, pl.ds(r, 1), :]
        atom_of = [flat[held * batches + b] for b in range(batches)]
        for k in range(held):
            sums = []
            for a in range(natoms):
                total = jnp.zeros((devices, radial), F32)
                for b in range(batches):
                    total = total + jnp.where(atom_of[b] == float(a), flat[k * batches + b], 0.0)
                sums.append(jnp.sum(total, axis=0, keepdims=True))
            atom_mom = jnp.concatenate(sums, axis=0)
            solved = lax.dot_general(
                atom_mom,
                green_ref[deg[k]],
                NT,
                precision=lax.Precision.HIGHEST,
                preferred_element_type=F32,
            )
            for b in range(batches):
                picked = jnp.zeros((devices, radial), F32)
                for a in range(natoms):
                    picked = jnp.where(atom_of[b] == float(a), solved[a : a + 1, :], picked)
                for d in range(devices):
                    out[d, pl.ds(b * held + k, 1), :] = picked[d : d + 1, :]
            for own in range(ATOM_COL):
                for d in range(devices):
                    a = (d % cols_count) * ATOM_COL + own
                    out[d, pl.ds((batches + own) * held + k, 1), :] = solved[a : a + 1, :]

    return pl.pallas_call(
        body,
        out_shape=jax.ShapeDtypeStruct((devices, rows_out, radial), F32),
        grid_spec=pltpu.PrefetchScalarGridSpec(
            num_scalar_prefetch=1,
            grid=(1,),
            in_specs=[full(arrived.shape), full(green.shape)],
            out_specs=full((devices, rows_out, radial)),
            scratch_shapes=[pltpu.VMEM((lines, devices, radial), F32)],
        ),
        compiler_params=params(16),
        name="radial_solve",
    )(degree_ids, arrived, green)


def potential_pass(active, slots, poles, rho, basis_t, harmonics, weights, shells, slot_count, blk, held):
    batches, span, points = basis_t.shape
    blocks = span // blk
    rows = harmonics.shape[1]
    devices, lines, radial = poles.shape
    chunk = min(512, points)
    wide = 2 * blk if blocks % 2 == 0 else blk

    def body(act, slot_ids, got, rho_ref, phi, harm, wts, shell, out, scaled, poles_keep):
        batch = pl.program_id(0)
        count = act[batch]

        @pl.when(batch == 0)
        def _():
            out[...] = jnp.zeros_like(out)

        for b in range(batches):

            @pl.when(batch == b)
            def _(b=b):
                for k in range(held):
                    for d in range(devices):
                        line = d * held + k
                        if line < rows:
                            poles_keep[pl.ds(line, 1), :] = got[d, pl.ds(b * held + k, 1), :]

        if held * devices < rows:
            poles_keep[pl.ds(held * devices, rows - held * devices), :] = jnp.zeros(
                (rows - held * devices, radial), F32
            )
        stacked = split3(poles_keep[...])

        def step(at, carry):
            cols = pl.ds(pl.multiple_of(at * chunk, chunk), chunk)
            ids = lax.broadcasted_iota(jnp.int32, (radial, chunk), 0)
            onehot = jnp.where(shell[0, :, cols] == ids, 1.0, 0.0).astype(BF16)
            at_points = join3(jnp.dot(stacked, onehot, preferred_element_type=F32))
            hartree = jnp.sum(harm[0, :, cols] * at_points, axis=0, keepdims=True)
            rho_c = rho_ref[0, :, cols]
            root = jnp.exp(jnp.log(1.0 + rho_c * rho_c) * (-1.0 / 3.0))
            factor = wts[0, :, cols] * (hartree - rho_c * root)
            scaled[:, cols] = (phi[0, :, cols].astype(F32) * factor).astype(BF16)
            return carry

        lax.fori_loop(0, points // chunk, step, 0)

        for first in range(0, span, wide):
            piece = lax.dot_general(
                phi[0], scaled[pl.ds(first, wide), :], NT, preferred_element_type=F32
            )
            for i in range(blocks):
                for j in range(first // blk, (first + wide) // blk):

                    @pl.when((i < count) & (j < count))
                    def _(i=i, j=j, piece=piece, first=first):
                        slot = jnp.clip(slot_ids[batch, i * blocks + j], 0, slot_count - 1)
                        left = j * blk - first
                        out[slot] = piece[i * blk : (i + 1) * blk, left : left + blk].astype(BF16)

    return pl.pallas_call(
        body,
        out_shape=jax.ShapeDtypeStruct((slot_count, blk, blk), BF16),
        grid_spec=pltpu.PrefetchScalarGridSpec(
            num_scalar_prefetch=2,
            grid=(batches,),
            in_specs=[
                full(poles.shape),
                pl.BlockSpec((1, 1, points), lambda b, *_: (b, 0, 0)),
                pl.BlockSpec((1, span, points), lambda b, *_: (b, 0, 0)),
                pl.BlockSpec((1, rows, points), lambda b, *_: (b, 0, 0)),
                pl.BlockSpec((1, 1, points), lambda b, *_: (b, 0, 0)),
                pl.BlockSpec((1, 1, points), lambda b, *_: (b, 0, 0)),
            ],
            out_specs=full((slot_count, blk, blk)),
            scratch_shapes=[pltpu.VMEM((span, points), BF16), pltpu.VMEM((rows, radial), F32)],
        ),
        compiler_params=params(32),
        name="potential_pass",
    )(active, slots, poles, rho, basis_t, harmonics, weights, shells)


def exchange(parts):
    return lax.all_to_all(parts, AXES, split_axis=0, concat_axis=0, tiled=True)


def shards(
    density_tiles,
    send_list,
    basis_values,
    active_blocks,
    touch_slots,
    point_weights,
    harmonics,
    shell_index,
    batch_atom,
    radial_green,
):
    devices = lax.axis_size(AXES)
    cols_count = lax.axis_size("col")
    capacity = send_list.shape[2]
    tiles_dev, blk, _ = density_tiles.shape
    batches, points, span = basis_values.shape
    harm_count = harmonics.shape[1]
    radial = radial_green.shape[1]
    slot_count = devices * capacity
    natoms = ATOM_COL * cols_count
    held = -(-harm_count // devices)
    rows = -(-harm_count // 16) * 16

    tile_ids = send_list.reshape(-1)
    outgoing = gather_tiles(tile_ids, density_tiles)
    arrived = exchange(outgoing.reshape(devices, capacity, blk, blk))
    received = arrived.reshape(slot_count, blk, blk)

    basis_t = jnp.transpose(basis_values, (0, 2, 1))
    harm_rows = jnp.pad(harmonics, ((0, 0), (0, rows - harm_count), (0, 0)))
    weights = point_weights[:, None, :]
    shells = shell_index[:, None, :]
    slots = touch_slots.reshape(batches, -1)

    rho, mom_out = density_pass(
        active_blocks, slots, batch_atom, received, basis_t, harm_rows, weights, shells,
        (held, radial), devices,
    )
    mom_in = exchange(mom_out)
    first = lax.axis_index(AXES) * held
    degree_ids = degrees(jnp.minimum(first + jnp.arange(held), harm_count - 1))
    poles_out = radial_solve(
        degree_ids, mom_in, radial_green, natoms, held, batches, cols_count
    )
    poles = exchange(poles_out)
    returning = potential_pass(
        active_blocks, slots, poles, rho, basis_t, harm_rows, weights, shells,
        slot_count, blk, held,
    )
    back = exchange(returning.reshape(devices, capacity, blk, blk))
    ham_tiles = sum_tiles(tile_ids, back.reshape(slot_count, blk, blk), tiles_dev)

    own = poles[:, batches * held :, :].reshape(devices, ATOM_COL, held, radial)
    own = jnp.transpose(own, (1, 0, 2, 3)).reshape(ATOM_COL, devices * held, radial)
    return (ham_tiles, own[:, :harm_count])


def solution(mesh):
    in_specs = (
        P(AXES, None, None),
        P(AXES, None, None),
        P(AXES, None, None),
        P(AXES),
        P(AXES, None, None),
        P(AXES, None),
        P(AXES, None, None),
        P(AXES, None),
        P(AXES),
        P(),
    )
    out_specs = (P(AXES, None, None), P("col", None, None))
    return jax.shard_map(shards, mesh=mesh, in_specs=in_specs, out_specs=out_specs, check_vma=False)
```

```python
import jax
import jax.numpy as jnp
from jax import lax
from jax.experimental import pallas as pl
from jax.experimental.pallas import tpu as pltpu
from jax.sharding import PartitionSpec as P

LDEG = 7
ATOM_COL = 2
AXES = ("row", "col")
F32 = jnp.float32
BF16 = jnp.bfloat16
NT = (((1,), (1,)), ((), ()))


def degrees(harm_ids):
    bounds = jnp.arange(1, LDEG) ** 2
    return jnp.sum((harm_ids[:, None] >= bounds[None, :]).astype(jnp.int32), axis=1)


SMEM = pl.BlockSpec(memory_space=pltpu.SMEM)
VMEM = pl.BlockSpec(memory_space=pltpu.VMEM)
HBM = pl.BlockSpec(memory_space=pltpu.HBM)


def params(mib):
    return pltpu.CompilerParams(vmem_limit_bytes=int(mib * 1024 * 1024))


def split2(values):
    high = values.astype(BF16)
    low = (values - high.astype(F32)).astype(BF16)
    return jnp.concatenate([high, low], axis=0)


def join2(stacked):
    rows = stacked.shape[0] // 2
    return stacked[:rows] + stacked[rows:]


def column_copies(source, held, sems, chunk):
    batches, _, points = source.shape
    pieces = points // chunk
    return [
        [
            pltpu.make_async_copy(
                source.at[b, :, pl.ds(c * chunk, chunk)],
                held.at[b, :, pl.ds(c * chunk, chunk)],
                sems.at[b * pieces + c],
            )
            for c in range(pieces)
        ]
        for b in range(batches)
    ]


def gather_tiles(tile_ids, tiles):
    capacity, devices = tile_ids.shape
    count = capacity * devices

    def body(ids, tiles_ref, out_ref, keep, sems):
        load = pltpu.make_async_copy(tiles_ref, keep, sems.at[0])
        load.start()
        load.wait()

        def send(dev, carry):
            for k in range(capacity):
                pltpu.make_async_copy(
                    keep.at[ids[k, dev]], out_ref.at[dev * capacity + k], sems.at[1]
                ).start()
            return carry

        lax.fori_loop(0, devices, send, 0, unroll=4)
        pltpu.make_async_copy(out_ref, out_ref, sems.at[1]).wait()

    return pl.pallas_call(
        body,
        out_shape=jax.ShapeDtypeStruct((count,) + tiles.shape[1:], tiles.dtype),
        in_specs=[SMEM, HBM],
        out_specs=HBM,
        scratch_shapes=[pltpu.VMEM(tiles.shape, tiles.dtype), pltpu.SemaphoreType.DMA((2,))],
        compiler_params=params(63),
        name="gather_tiles",
    )(tile_ids, tiles)


def sum_tiles(tile_ids, arrived, tiles_dev):
    capacity, devices = tile_ids.shape
    _, blk, _ = arrived.shape

    def body(ids, arrived_ref, out_ref):
        out_ref[...] = jnp.zeros_like(out_ref)

        def add(dev, carry):
            for k in range(capacity):
                tile = ids[k, dev]
                out_ref[tile] = out_ref[tile] + arrived_ref[dev * capacity + k].astype(F32)
            return carry

        lax.fori_loop(0, devices, add, 0, unroll=4)

    return pl.pallas_call(
        body,
        out_shape=jax.ShapeDtypeStruct((tiles_dev, blk, blk), F32),
        in_specs=[SMEM, VMEM],
        out_specs=VMEM,
        compiler_params=params(16),
        name="sum_tiles",
    )(tile_ids, arrived)


def density_pass(active, slots, atoms, received, basis_t, harmonics, weights, shells, share, devices):
    batches, span, points = basis_t.shape
    slot_count, blk, _ = received.shape
    blocks = span // blk
    rows = harmonics.shape[1]
    held, radial = share
    chunk = points
    pieces = points // chunk
    lines = (held + 1) * batches

    def body(act, slot_ids, atom_ids, recv, phi_hbm, harm_hbm, wts, shell, rho_out, send,
             phi, harm, matrix, mom_keep, sems, harm_sem):
        copies = column_copies(phi_hbm, phi, sems, chunk)
        harm_copy = pltpu.make_async_copy(harm_hbm, harm, harm_sem)
        for b in range(batches):
            for copy in copies[b]:
                copy.start()
            if b == 0:
                harm_copy.start()

        for b in range(batches):
            count = act[b]
            for i in range(blocks):
                for j in range(blocks):
                    spot = (b, pl.ds(i * blk, blk), pl.ds(j * blk, blk))
                    live = (i < count) & (j < count)

                    @pl.when(live)
                    def _(b=b, i=i, j=j, spot=spot):
                        slot = jnp.clip(slot_ids[b, i * blocks + j], 0, slot_count - 1)
                        matrix[spot] = recv[slot]

                    @pl.when(jnp.logical_not(live))
                    def _(spot=spot):
                        matrix[spot] = jnp.zeros((blk, blk), BF16)

        for b in range(batches):
            send[:, pl.ds(held * batches + b, 1), :] = jnp.full(
                (devices, 1, radial), atom_ids[b].astype(F32), F32
            )

        def moments(b):
            weighted = harm[b] * (wts[b] * rho_out[b])
            ids = lax.broadcasted_iota(jnp.int32, (radial, points), 0)
            onehot = jnp.where(shell[b] == ids, 1.0, 0.0).astype(BF16)
            mom_keep[b] = join2(
                lax.dot_general(split2(weighted), onehot, NT, preferred_element_type=F32)
            )
            for k in range(held):
                for d in range(devices):
                    line = d * held + k
                    if line < rows:
                        send[d, pl.ds(k * batches + b, 1), :] = mom_keep[b, pl.ds(line, 1), :]
                    else:
                        send[d, pl.ds(k * batches + b, 1), :] = jnp.zeros((1, radial), F32)

        for b in range(batches):
            for c in range(pieces):
                copies[b][c].wait()
                cols = pl.ds(c * chunk, chunk)
                phi_c = phi[b, :, cols]
                product = jnp.dot(matrix[b], phi_c, preferred_element_type=F32)
                rho_out[b, :, cols] = jnp.sum(
                    product * phi_c.astype(F32), axis=0, keepdims=True
                )
            if b == 0:
                harm_copy.wait()

        for b in range(batches):
            moments(b)

    return pl.pallas_call(
        body,
        out_shape=(
            jax.ShapeDtypeStruct((batches, 1, points), F32),
            jax.ShapeDtypeStruct((devices, lines, radial), F32),
        ),
        in_specs=[SMEM, SMEM, SMEM, VMEM, HBM, HBM, VMEM, VMEM],
        out_specs=(VMEM, VMEM),
        scratch_shapes=[
            pltpu.VMEM(basis_t.shape, BF16),
            pltpu.VMEM(harmonics.shape, F32),
            pltpu.VMEM((batches, span, span), BF16),
            pltpu.VMEM((batches, rows, radial), F32),
            pltpu.SemaphoreType.DMA((batches * pieces,)),
            pltpu.SemaphoreType.DMA,
        ],
        compiler_params=params(54 - received.size * 2 / 2**20),
        name="density_pass",
    )(active, slots, atoms, received, basis_t, harmonics, weights, shells)


def radial_solve(degree_ids, arrived, green, natoms, held, batches, cols_count):
    devices, lines, radial = arrived.shape
    rows_out = (batches + ATOM_COL) * held

    def body(deg, got, green_hbm, out, flat, green, sems):
        loads = [
            pltpu.make_async_copy(green_hbm.at[deg[k]], green.at[k], sems.at[k])
            for k in range(held)
        ]
        for load in loads:
            load.start()
        for r in range(lines):
            for d in range(devices):
                flat[r, pl.ds(d, 1), :] = got[d, pl.ds(r, 1), :]
        atom_of = [flat[held * batches + b] for b in range(batches)]
        for k in range(held):
            sums = []
            for a in range(natoms):
                total = jnp.zeros((devices, radial), F32)
                for b in range(batches):
                    total = total + jnp.where(atom_of[b] == float(a), flat[k * batches + b], 0.0)
                sums.append(jnp.sum(total, axis=0, keepdims=True))
            atom_mom = jnp.concatenate(sums, axis=0)
            loads[k].wait()
            solved = lax.dot_general(
                atom_mom,
                green[k],
                NT,
                precision=lax.Precision.HIGHEST,
                preferred_element_type=F32,
            )
            for b in range(batches):
                picked = jnp.zeros((devices, radial), F32)
                for a in range(natoms):
                    picked = jnp.where(atom_of[b] == float(a), solved[a : a + 1, :], picked)
                for d in range(devices):
                    out[d, pl.ds(b * held + k, 1), :] = picked[d : d + 1, :]
            for own in range(ATOM_COL):
                for d in range(devices):
                    a = (d % cols_count) * ATOM_COL + own
                    out[d, pl.ds((batches + own) * held + k, 1), :] = solved[a : a + 1, :]

    return pl.pallas_call(
        body,
        out_shape=jax.ShapeDtypeStruct((devices, rows_out, radial), F32),
        in_specs=[SMEM, VMEM, HBM],
        out_specs=VMEM,
        scratch_shapes=[
            pltpu.VMEM((lines, devices, radial), F32),
            pltpu.VMEM((held, radial, radial), F32),
            pltpu.SemaphoreType.DMA((held,)),
        ],
        compiler_params=params(53.5),
        name="radial_solve",
    )(degree_ids, arrived, green)


def potential_pass(active, slots, poles, rho, basis_t, harmonics, weights, shells, slot_count, blk, held):
    batches, span, points = basis_t.shape
    blocks = span // blk
    rows = harmonics.shape[1]
    devices, lines, radial = poles.shape
    chunk = points
    pieces = points // chunk
    wide = 2 * blk if blocks % 2 == 0 else blk

    def body(act, slot_ids, got, rho_ref, phi_hbm, harm_hbm, wts, shell, out,
             phi, harm, scaled, poles_keep, sems, harm_sem):
        copies = column_copies(phi_hbm, phi, sems, chunk)
        harm_copy = pltpu.make_async_copy(harm_hbm, harm, harm_sem)
        harm_copy.start()
        for b in range(batches):
            for copy in copies[b]:
                copy.start()

        out[...] = jnp.zeros_like(out)
        if held * devices < rows:
            poles_keep[...] = jnp.zeros_like(poles_keep)
        for b in range(batches):
            for k in range(held):
                for d in range(devices):
                    line = d * held + k
                    if line < rows:
                        poles_keep[b, pl.ds(line, 1), :] = got[d, pl.ds(b * held + k, 1), :]
        harm_copy.wait()

        for b in range(batches):
            stacked = split2(poles_keep[b])
            for c in range(pieces):
                copies[b][c].wait()
                cols = pl.ds(c * chunk, chunk)
                ids = lax.broadcasted_iota(jnp.int32, (radial, chunk), 0)
                onehot = jnp.where(shell[b, :, cols] == ids, 1.0, 0.0).astype(BF16)
                at_points = join2(jnp.dot(stacked, onehot, preferred_element_type=F32))
                hartree = jnp.sum(harm[b, :, cols] * at_points, axis=0, keepdims=True)
                rho_c = rho_ref[b, :, cols]
                root = jnp.exp(jnp.log(1.0 + rho_c * rho_c) * (-1.0 / 3.0))
                factor = wts[b, :, cols] * (hartree - rho_c * root)
                scaled[b, :, cols] = (phi[b, :, cols].astype(F32) * factor).astype(BF16)

        for b in range(batches):
            count = act[b]
            for first in range(0, span, wide):
                piece = lax.dot_general(
                    phi[b], scaled[b, pl.ds(first, wide), :], NT, preferred_element_type=F32
                )
                for i in range(blocks):
                    for j in range(first // blk, (first + wide) // blk):
                        live = (i < count) & (j < count)
                        slot = jnp.clip(slot_ids[b, i * blocks + j], 0, slot_count - 1)
                        left = j * blk - first
                        tile = piece[i * blk : (i + 1) * blk, left : left + blk].astype(BF16)
                        out[slot] = jnp.where(live, tile, out[slot])

    return pl.pallas_call(
        body,
        out_shape=jax.ShapeDtypeStruct((slot_count, blk, blk), BF16),
        in_specs=[SMEM, SMEM, VMEM, VMEM, HBM, HBM, VMEM, VMEM],
        out_specs=VMEM,
        scratch_shapes=[
            pltpu.VMEM(basis_t.shape, BF16),
            pltpu.VMEM(harmonics.shape, F32),
            pltpu.VMEM(basis_t.shape, BF16),
            pltpu.VMEM((batches, rows, radial), F32),
            pltpu.SemaphoreType.DMA((batches * pieces,)),
            pltpu.SemaphoreType.DMA,
        ],
        compiler_params=params(62),
        name="potential_pass",
    )(active, slots, poles, rho, basis_t, harmonics, weights, shells)


def exchange(parts):
    return lax.all_to_all(parts, AXES, split_axis=0, concat_axis=0, tiled=True)


def shards(
    density_tiles,
    send_list,
    basis_values,
    active_blocks,
    touch_slots,
    point_weights,
    harmonics,
    shell_index,
    batch_atom,
    radial_green,
):
    devices = lax.axis_size(AXES)
    cols_count = lax.axis_size("col")
    capacity = send_list.shape[2]
    tiles_dev, blk, _ = density_tiles.shape
    batches, points, span = basis_values.shape
    harm_count = harmonics.shape[1]
    radial = radial_green.shape[1]
    slot_count = devices * capacity
    natoms = ATOM_COL * cols_count
    held = -(-harm_count // devices)
    rows = -(-harm_count // 16) * 16

    tile_ids = jnp.transpose(send_list, (2, 0, 1)).reshape(capacity, devices)
    outgoing = gather_tiles(tile_ids, density_tiles)
    arrived = exchange(outgoing.reshape(devices, capacity, blk, blk))
    received = arrived.reshape(slot_count, blk, blk)

    basis_t = jnp.transpose(basis_values, (0, 2, 1))
    harm_rows = jnp.pad(harmonics, ((0, 0), (0, rows - harm_count), (0, 0)))
    weights = point_weights[:, None, :]
    shells = shell_index[:, None, :]
    slots = touch_slots.reshape(batches, -1)

    rho, mom_out = density_pass(
        active_blocks, slots, batch_atom, received, basis_t, harm_rows, weights, shells,
        (held, radial), devices,
    )
    mom_in = exchange(mom_out)
    first = lax.axis_index(AXES) * held
    degree_ids = degrees(jnp.minimum(first + jnp.arange(held), harm_count - 1))
    poles_out = radial_solve(
        degree_ids, mom_in, radial_green, natoms, held, batches, cols_count
    )
    poles = exchange(poles_out)
    returning = potential_pass(
        active_blocks, slots, poles, rho, basis_t, harm_rows, weights, shells,
        slot_count, blk, held,
    )
    back = exchange(returning.reshape(devices, capacity, blk, blk))
    ham_tiles = sum_tiles(tile_ids, back.reshape(slot_count, blk, blk), tiles_dev)

    own = poles[:, batches * held :, :].reshape(devices, ATOM_COL, held, radial)
    own = jnp.transpose(own, (1, 0, 2, 3)).reshape(ATOM_COL, devices * held, radial)
    return (ham_tiles, own[:, :harm_count])


def solution(mesh):
    in_specs = (
        P(AXES, None, None),
        P(AXES, None, None),
        P(AXES, None, None),
        P(AXES),
        P(AXES, None, None),
        P(AXES, None),
        P(AXES, None, None),
        P(AXES, None),
        P(AXES),
        P(),
    )
    out_specs = (P(AXES, None, None), P("col", None, None))
    return jax.shard_map(shards, mesh=mesh, in_specs=in_specs, out_specs=out_specs, check_vma=False)
```

```python
import jax
import jax.numpy as jnp
from jax import lax
from jax.experimental import pallas as pl
from jax.experimental.pallas import tpu as pltpu
from jax.sharding import PartitionSpec as P

LDEG = 7
ATOM_COL = 2
AXES = ("row", "col")
F32 = jnp.float32
BF16 = jnp.bfloat16
NT = (((1,), (1,)), ((), ()))
SPARE = 256


def degrees(harm_ids):
    bounds = jnp.arange(1, LDEG) ** 2
    return jnp.sum((harm_ids[:, None] >= bounds[None, :]).astype(jnp.int32), axis=1)


SMEM = pl.BlockSpec(memory_space=pltpu.SMEM)
VMEM = pl.BlockSpec(memory_space=pltpu.VMEM)
HBM = pl.BlockSpec(memory_space=pltpu.HBM)


def params(mib):
    return pltpu.CompilerParams(vmem_limit_bytes=int(mib * 1024 * 1024))


def split2(values):
    high = values.astype(BF16)
    low = (values - high.astype(F32)).astype(BF16)
    return jnp.concatenate([high, low], axis=0)


def join2(stacked):
    rows = stacked.shape[0] // 2
    return stacked[:rows] + stacked[rows:]


def loads_of(source, held, sems):
    return [
        pltpu.make_async_copy(source.at[b], held.at[b], sems.at[b])
        for b in range(sems.shape[0])
    ]


def gather_tiles(tile_ids, tiles):
    capacity, _, devices = tile_ids.shape
    count = capacity * devices

    def body(ids, tiles_ref, out_ref, keep, sems):
        load = pltpu.make_async_copy(tiles_ref, keep, sems.at[0])
        load.start()
        load.wait()

        def send(dev, carry):
            for k in range(capacity):
                pltpu.make_async_copy(
                    keep.at[ids[k, 0, dev]], out_ref.at[dev * capacity + k], sems.at[1]
                ).start()
            return carry

        lax.fori_loop(0, devices, send, 0, unroll=4)
        pltpu.make_async_copy(out_ref, out_ref, sems.at[1]).wait()

    return pl.pallas_call(
        body,
        out_shape=jax.ShapeDtypeStruct((count,) + tiles.shape[1:], tiles.dtype),
        in_specs=[SMEM, HBM],
        out_specs=HBM,
        scratch_shapes=[pltpu.VMEM(tiles.shape, tiles.dtype), pltpu.SemaphoreType.DMA((2,))],
        compiler_params=params(63),
        name="gather_tiles",
    )(tile_ids, tiles)


def sum_tiles(tile_ids, arrived, tiles_dev):
    capacity, _, devices = tile_ids.shape
    _, blk, _ = arrived.shape

    def body(ids, arrived_ref, out_ref):
        out_ref[...] = jnp.zeros_like(out_ref)

        def add(dev, carry):
            for k in range(capacity):
                tile = ids[k, 0, dev]
                out_ref[tile] = out_ref[tile] + arrived_ref[dev * capacity + k].astype(F32)
            return carry

        lax.fori_loop(0, devices, add, 0, unroll=4)

    return pl.pallas_call(
        body,
        out_shape=jax.ShapeDtypeStruct((tiles_dev, blk, blk), F32),
        in_specs=[SMEM, VMEM],
        out_specs=VMEM,
        compiler_params=params(16),
        name="sum_tiles",
    )(tile_ids, arrived)


def density_pass(active, slots, atoms, received, basis_t, harmonics, weights, shells, share, devices):
    batches, span, points = basis_t.shape
    slot_count, blk, _ = received.shape
    blocks = span // blk
    rows = harmonics.shape[1]
    held, radial = share
    lines = (held + 1) * batches

    def body(act, slot_ids, atom_ids, recv, phi_hbm, harm_hbm, wts, shell, rho_hbm, send,
             phi, harm, rho, matrix, mom_keep, phi_sems, harm_sems, rho_sems):
        phi_loads = loads_of(phi_hbm, phi, phi_sems)
        harm_loads = loads_of(harm_hbm, harm, harm_sems)
        rho_stores = loads_of(rho, rho_hbm, rho_sems)
        for load in phi_loads + harm_loads:
            load.start()

        for b in range(batches):
            count = act[b]
            for i in range(blocks):
                for j in range(blocks):
                    spot = (b, pl.ds(i * blk, blk), pl.ds(j * blk, blk))
                    live = (i < count) & (j < count)

                    @pl.when(live)
                    def _(b=b, i=i, j=j, spot=spot):
                        slot = jnp.clip(slot_ids[b, i * blocks + j], 0, slot_count - 1)
                        matrix[spot] = recv[slot]

                    @pl.when(jnp.logical_not(live))
                    def _(spot=spot):
                        matrix[spot] = jnp.zeros((blk, blk), BF16)

        for b in range(batches):
            send[:, pl.ds(held * batches + b, 1), :] = jnp.full(
                (devices, 1, radial), atom_ids[b].astype(F32), F32
            )

        def moments(b):
            weighted = harm[b] * (wts[b] * rho[b])
            ids = lax.broadcasted_iota(jnp.int32, (radial, points), 0)
            onehot = jnp.where(shell[b] == ids, 1.0, 0.0).astype(BF16)
            mom_keep[b] = join2(
                lax.dot_general(split2(weighted), onehot, NT, preferred_element_type=F32)
            )
            for k in range(held):
                for d in range(devices):
                    line = d * held + k
                    if line < rows:
                        send[d, pl.ds(k * batches + b, 1), :] = mom_keep[b, pl.ds(line, 1), :]
                    else:
                        send[d, pl.ds(k * batches + b, 1), :] = jnp.zeros((1, radial), F32)

        for b in range(batches):
            phi_loads[b].wait()
            product = jnp.dot(matrix[b], phi[b], preferred_element_type=F32)
            rho[b] = jnp.sum(product * phi[b].astype(F32), axis=0, keepdims=True)
            rho_stores[b].start()

        for b in range(batches):
            harm_loads[b].wait()
            moments(b)
        for store in rho_stores:
            store.wait()

    return pl.pallas_call(
        body,
        out_shape=(
            jax.ShapeDtypeStruct((SPARE * batches, 1, points), F32),
            jax.ShapeDtypeStruct((devices, lines, radial), F32),
        ),
        in_specs=[SMEM, SMEM, SMEM, VMEM, HBM, HBM, VMEM, VMEM],
        out_specs=(HBM, VMEM),
        scratch_shapes=[
            pltpu.VMEM(basis_t.shape, BF16),
            pltpu.VMEM((batches, rows, points), F32),
            pltpu.VMEM((batches, 1, points), F32),
            pltpu.VMEM((batches, span, span), BF16),
            pltpu.VMEM((batches, rows, radial), F32),
            pltpu.SemaphoreType.DMA((batches,)),
            pltpu.SemaphoreType.DMA((batches,)),
            pltpu.SemaphoreType.DMA((batches,)),
        ],
        compiler_params=params(52 - received.size * 2 / 2**20),
        name="density_pass",
    )(active, slots, atoms, received, basis_t, harmonics, weights, shells)


def radial_solve(degree_ids, arrived, green, natoms, held, batches, cols_count):
    devices, lines, radial = arrived.shape
    rows_out = (batches + ATOM_COL) * held

    def body(deg, got, green_hbm, out, flat, green, sems):
        loads = [
            pltpu.make_async_copy(green_hbm.at[deg[k]], green.at[k], sems.at[k])
            for k in range(held)
        ]
        for load in loads:
            load.start()
        for r in range(lines):
            for d in range(devices):
                flat[r, pl.ds(d, 1), :] = got[d, pl.ds(r, 1), :]
        atom_of = [flat[held * batches + b] for b in range(batches)]
        for k in range(held):
            sums = []
            for a in range(natoms):
                total = jnp.zeros((devices, radial), F32)
                for b in range(batches):
                    total = total + jnp.where(atom_of[b] == float(a), flat[k * batches + b], 0.0)
                sums.append(jnp.sum(total, axis=0, keepdims=True))
            atom_mom = jnp.concatenate(sums, axis=0)
            loads[k].wait()
            solved = lax.dot_general(
                atom_mom,
                green[k],
                NT,
                precision=lax.Precision.HIGHEST,
                preferred_element_type=F32,
            )
            for b in range(batches):
                picked = jnp.zeros((devices, radial), F32)
                for a in range(natoms):
                    picked = jnp.where(atom_of[b] == float(a), solved[a : a + 1, :], picked)
                for d in range(devices):
                    out[d, pl.ds(b * held + k, 1), :] = picked[d : d + 1, :]
            for own in range(ATOM_COL):
                for d in range(devices):
                    a = (d % cols_count) * ATOM_COL + own
                    out[d, pl.ds((batches + own) * held + k, 1), :] = solved[a : a + 1, :]

    return pl.pallas_call(
        body,
        out_shape=jax.ShapeDtypeStruct((devices, rows_out, radial), F32),
        in_specs=[SMEM, VMEM, HBM],
        out_specs=VMEM,
        scratch_shapes=[
            pltpu.VMEM((lines, devices, radial), F32),
            pltpu.VMEM((held, radial, radial), F32),
            pltpu.SemaphoreType.DMA((held,)),
        ],
        compiler_params=params(53.5),
        name="radial_solve",
    )(degree_ids, arrived, green)


def potential_pass(active, slots, poles, rho, basis_t, harmonics, weights, shells, slot_count, blk, held):
    batches, span, points = basis_t.shape
    blocks = span // blk
    rows = harmonics.shape[1]
    devices, lines, radial = poles.shape
    wide = 2 * blk if blocks % 2 == 0 else blk

    def body(act, slot_ids, got, rho_hbm, phi_hbm, harm_hbm, wts, shell, out,
             phi, harm, rho, scaled, poles_keep, phi_sems, harm_sems, rho_sems):
        phi_loads = loads_of(phi_hbm, phi, phi_sems)
        harm_loads = loads_of(harm_hbm, harm, harm_sems)
        rho_loads = loads_of(rho_hbm, rho, rho_sems)
        for load in rho_loads + harm_loads + phi_loads:
            load.start()

        out[...] = jnp.zeros_like(out)
        if held * devices < rows:
            poles_keep[...] = jnp.zeros_like(poles_keep)
        for b in range(batches):
            for k in range(held):
                for d in range(devices):
                    line = d * held + k
                    if line < rows:
                        poles_keep[b, pl.ds(line, 1), :] = got[d, pl.ds(b * held + k, 1), :]

        factors = []
        for b in range(batches):
            rho_loads[b].wait()
            harm_loads[b].wait()
            ids = lax.broadcasted_iota(jnp.int32, (radial, points), 0)
            onehot = jnp.where(shell[b] == ids, 1.0, 0.0).astype(BF16)
            at_points = join2(
                jnp.dot(split2(poles_keep[b]), onehot, preferred_element_type=F32)
            )
            hartree = jnp.sum(harm[b] * at_points, axis=0, keepdims=True)
            root = jnp.exp(jnp.log(1.0 + rho[b] * rho[b]) * (-1.0 / 3.0))
            factors.append(wts[b] * (hartree - rho[b] * root))

        for b in range(batches):
            phi_loads[b].wait()
            scaled[b] = (phi[b].astype(F32) * factors[b]).astype(BF16)

        for b in range(batches):
            count = act[b]
            for first in range(0, span, wide):
                piece = lax.dot_general(
                    phi[b], scaled[b, pl.ds(first, wide), :], NT, preferred_element_type=F32
                )
                for i in range(blocks):
                    for j in range(first // blk, (first + wide) // blk):
                        live = (i < count) & (j < count)
                        slot = jnp.clip(slot_ids[b, i * blocks + j], 0, slot_count - 1)
                        left = j * blk - first
                        tile = piece[i * blk : (i + 1) * blk, left : left + blk].astype(BF16)
                        out[slot] = jnp.where(live, tile, out[slot])

    return pl.pallas_call(
        body,
        out_shape=jax.ShapeDtypeStruct((slot_count, blk, blk), BF16),
        in_specs=[SMEM, SMEM, VMEM, VMEM, HBM, HBM, VMEM, VMEM],
        out_specs=VMEM,
        scratch_shapes=[
            pltpu.VMEM(basis_t.shape, BF16),
            pltpu.VMEM((batches, rows, points), F32),
            pltpu.VMEM((batches, 1, points), F32),
            pltpu.VMEM(basis_t.shape, BF16),
            pltpu.VMEM((batches, rows, radial), F32),
            pltpu.SemaphoreType.DMA((batches,)),
            pltpu.SemaphoreType.DMA((batches,)),
            pltpu.SemaphoreType.DMA((batches,)),
        ],
        compiler_params=params(62),
        name="potential_pass",
    )(active, slots, poles, rho, basis_t, harmonics, weights, shells)


def exchange(parts):
    return lax.all_to_all(parts, AXES, split_axis=0, concat_axis=0, tiled=True)


def shards(
    density_tiles,
    send_list,
    basis_values,
    active_blocks,
    touch_slots,
    point_weights,
    harmonics,
    shell_index,
    batch_atom,
    radial_green,
):
    devices = lax.axis_size(AXES)
    cols_count = lax.axis_size("col")
    capacity = send_list.shape[2]
    tiles_dev, blk, _ = density_tiles.shape
    batches, points, span = basis_values.shape
    harm_count = harmonics.shape[1]
    radial = radial_green.shape[1]
    slot_count = devices * capacity
    natoms = ATOM_COL * cols_count
    held = -(-harm_count // devices)
    rows = -(-harm_count // 16) * 16

    tile_ids = jnp.transpose(send_list, (2, 0, 1))
    outgoing = gather_tiles(tile_ids, density_tiles)
    arrived = exchange(outgoing.reshape(devices, capacity, blk, blk))
    received = arrived.reshape(slot_count, blk, blk)

    basis_t = jnp.transpose(basis_values, (0, 2, 1))
    harm_rows = jnp.pad(harmonics, ((0, 2 * batches), (0, rows - harm_count), (0, 0)))
    weights = point_weights[:, None, :]
    shells = shell_index[:, None, :]
    slots = touch_slots.reshape(batches, -1)

    rho, mom_out = density_pass(
        active_blocks, slots, batch_atom, received, basis_t, harm_rows, weights, shells,
        (held, radial), devices,
    )
    mom_in = exchange(mom_out)
    first = lax.axis_index(AXES) * held
    degree_ids = degrees(jnp.minimum(first + jnp.arange(held), harm_count - 1))
    poles_out = radial_solve(
        degree_ids, mom_in, radial_green, natoms, held, batches, cols_count
    )
    poles = exchange(poles_out)
    returning = potential_pass(
        active_blocks, slots, poles, rho, basis_t, harm_rows, weights, shells,
        slot_count, blk, held,
    )
    back = exchange(returning.reshape(devices, capacity, blk, blk))
    ham_tiles = sum_tiles(tile_ids, back.reshape(slot_count, blk, blk), tiles_dev)

    own = poles[:, batches * held :, :].reshape(devices, ATOM_COL, held, radial)
    own = jnp.transpose(own, (1, 0, 2, 3)).reshape(ATOM_COL, devices * held, radial)
    return (ham_tiles, own[:, :harm_count])


def solution(mesh):
    in_specs = (
        P(AXES, None, None),
        P(AXES, None, None),
        P(AXES, None, None),
        P(AXES),
        P(AXES, None, None),
        P(AXES, None),
        P(AXES, None, None),
        P(AXES, None),
        P(AXES),
        P(),
    )
    out_specs = (P(AXES, None, None), P("col", None, None))
    return jax.shard_map(shards, mesh=mesh, in_specs=in_specs, out_specs=out_specs, check_vma=False)
```

```python
import jax
import jax.numpy as jnp
from jax import lax
from jax.experimental import pallas as pl
from jax.experimental.pallas import tpu as pltpu
from jax.sharding import PartitionSpec as P

LDEG = 7
ATOM_COL = 2
AXES = ("row", "col")
F32 = jnp.float32
BF16 = jnp.bfloat16
NT = (((1,), (1,)), ((), ()))
SPARE = 256


def degrees(harm_ids):
    bounds = jnp.arange(1, LDEG) ** 2
    return jnp.sum((harm_ids[:, None] >= bounds[None, :]).astype(jnp.int32), axis=1)


SMEM = pl.BlockSpec(memory_space=pltpu.SMEM)
VMEM = pl.BlockSpec(memory_space=pltpu.VMEM)
HBM = pl.BlockSpec(memory_space=pltpu.HBM)


def params(mib):
    return pltpu.CompilerParams(vmem_limit_bytes=int(mib * 1024 * 1024))


def split2(values):
    high = values.astype(BF16)
    low = (values - high.astype(F32)).astype(BF16)
    return jnp.concatenate([high, low], axis=0)


def join2(stacked):
    rows = stacked.shape[0] // 2
    return stacked[:rows] + stacked[rows:]


def loads_of(source, held, sems):
    return [
        pltpu.make_async_copy(source.at[b], held.at[b], sems.at[b])
        for b in range(sems.shape[0])
    ]


def gather_tiles(tile_ids, tiles):
    capacity, _, devices = tile_ids.shape
    count = capacity * devices

    def body(ids, tiles_ref, out_ref, keep, sems):
        load = pltpu.make_async_copy(tiles_ref, keep, sems.at[0])
        load.start()
        load.wait()

        def send(dev, carry):
            for k in range(capacity):
                pltpu.make_async_copy(
                    keep.at[ids[k, 0, dev]], out_ref.at[dev * capacity + k], sems.at[1]
                ).start()
            return carry

        lax.fori_loop(0, devices, send, 0, unroll=4)
        pltpu.make_async_copy(out_ref, out_ref, sems.at[1]).wait()

    return pl.pallas_call(
        body,
        out_shape=jax.ShapeDtypeStruct((count,) + tiles.shape[1:], tiles.dtype),
        in_specs=[SMEM, HBM],
        out_specs=HBM,
        scratch_shapes=[pltpu.VMEM(tiles.shape, tiles.dtype), pltpu.SemaphoreType.DMA((2,))],
        compiler_params=params(63),
        name="gather_tiles",
    )(tile_ids, tiles)


def sum_tiles(tile_ids, arrived, tiles_dev):
    capacity, _, devices = tile_ids.shape
    _, blk, _ = arrived.shape

    def body(ids, arrived_ref, out_ref):
        out_ref[...] = jnp.zeros_like(out_ref)

        def add(dev, carry):
            for k in range(capacity):
                tile = ids[k, 0, dev]
                out_ref[tile] = out_ref[tile] + arrived_ref[dev * capacity + k].astype(F32)
            return carry

        lax.fori_loop(0, devices, add, 0, unroll=4)

    return pl.pallas_call(
        body,
        out_shape=jax.ShapeDtypeStruct((tiles_dev, blk, blk), F32),
        in_specs=[SMEM, VMEM],
        out_specs=VMEM,
        compiler_params=params(16),
        name="sum_tiles",
    )(tile_ids, arrived)


def density_pass(active, slots, atoms, received, basis_t, harmonics, weights, shells, share, devices):
    batches, span, points = basis_t.shape
    slot_count, blk, _ = received.shape
    blocks = span // blk
    rows = harmonics.shape[1]
    held, radial = share
    lines = (held + 1) * batches

    def body(act, slot_ids, atom_ids, recv, phi_hbm, harm_hbm, wts, shell, rho_hbm, send,
             phi, harm, rho, matrix, mom_keep, phi_sems, harm_sems, rho_sems):
        phi_loads = loads_of(phi_hbm, phi, phi_sems)
        harm_loads = loads_of(harm_hbm, harm, harm_sems)
        rho_stores = loads_of(rho, rho_hbm, rho_sems)
        for load in phi_loads + harm_loads:
            load.start()

        for b in range(batches):
            count = act[b]
            for i in range(blocks):
                for j in range(blocks):
                    spot = (b, pl.ds(i * blk, blk), pl.ds(j * blk, blk))
                    live = (i < count) & (j < count)

                    @pl.when(live)
                    def _(b=b, i=i, j=j, spot=spot):
                        slot = jnp.clip(slot_ids[b, i * blocks + j], 0, slot_count - 1)
                        matrix[spot] = recv[slot]

                    @pl.when(jnp.logical_not(live))
                    def _(spot=spot):
                        matrix[spot] = jnp.zeros((blk, blk), BF16)

        for b in range(batches):
            send[:, pl.ds(held * batches + b, 1), :] = jnp.full(
                (devices, 1, radial), atom_ids[b].astype(F32), F32
            )

        def moments(b):
            weighted = harm[b] * (wts[b] * rho[b])
            ids = lax.broadcasted_iota(jnp.int32, (radial, points), 0)
            onehot = jnp.where(shell[b] == ids, 1.0, 0.0).astype(BF16)
            mom_keep[b] = join2(
                lax.dot_general(split2(weighted), onehot, NT, preferred_element_type=F32)
            )
            for k in range(held):
                for d in range(devices):
                    line = d * held + k
                    if line < rows:
                        send[d, pl.ds(k * batches + b, 1), :] = mom_keep[b, pl.ds(line, 1), :]
                    else:
                        send[d, pl.ds(k * batches + b, 1), :] = jnp.zeros((1, radial), F32)

        for b in range(batches):
            phi_loads[b].wait()
            product = jnp.dot(matrix[b], phi[b], preferred_element_type=F32)
            rho[b] = jnp.sum(product * phi[b].astype(F32), axis=0, keepdims=True)
            rho_stores[b].start()

        for b in range(batches):
            harm_loads[b].wait()
            moments(b)
        for store in rho_stores:
            store.wait()

    return pl.pallas_call(
        body,
        out_shape=(
            jax.ShapeDtypeStruct((SPARE * batches, 1, points), F32),
            jax.ShapeDtypeStruct((devices, lines, radial), F32),
        ),
        in_specs=[SMEM, SMEM, SMEM, VMEM, HBM, HBM, VMEM, VMEM],
        out_specs=(HBM, VMEM),
        scratch_shapes=[
            pltpu.VMEM(basis_t.shape, BF16),
            pltpu.VMEM((batches, rows, points), F32),
            pltpu.VMEM((batches, 1, points), F32),
            pltpu.VMEM((batches, span, span), BF16),
            pltpu.VMEM((batches, rows, radial), F32),
            pltpu.SemaphoreType.DMA((batches,)),
            pltpu.SemaphoreType.DMA((batches,)),
            pltpu.SemaphoreType.DMA((batches,)),
        ],
        compiler_params=params(52 - received.size * 2 / 2**20),
        name="density_pass",
    )(active, slots, atoms, received, basis_t, harmonics, weights, shells)


def radial_solve(degree_ids, arrived, green, natoms, held, batches, cols_count):
    devices, lines, radial = arrived.shape
    rows_out = (batches + ATOM_COL) * held

    def body(deg, got, green_hbm, out, flat, green, sems):
        loads = [
            pltpu.make_async_copy(green_hbm.at[deg[k]], green.at[k], sems.at[k])
            for k in range(held)
        ]
        for load in loads:
            load.start()
        for r in range(lines):
            for d in range(devices):
                flat[r, pl.ds(d, 1), :] = got[d, pl.ds(r, 1), :]
        atom_of = [flat[held * batches + b] for b in range(batches)]
        for k in range(held):
            sums = []
            for a in range(natoms):
                total = jnp.zeros((devices, radial), F32)
                for b in range(batches):
                    total = total + jnp.where(atom_of[b] == float(a), flat[k * batches + b], 0.0)
                sums.append(jnp.sum(total, axis=0, keepdims=True))
            atom_mom = jnp.concatenate(sums, axis=0)
            loads[k].wait()
            solved = lax.dot_general(
                atom_mom,
                green[k],
                NT,
                precision=lax.Precision.HIGHEST,
                preferred_element_type=F32,
            )
            for b in range(batches):
                picked = jnp.zeros((devices, radial), F32)
                for a in range(natoms):
                    picked = jnp.where(atom_of[b] == float(a), solved[a : a + 1, :], picked)
                for d in range(devices):
                    out[d, pl.ds(b * held + k, 1), :] = picked[d : d + 1, :]
            for own in range(ATOM_COL):
                for d in range(devices):
                    a = (d % cols_count) * ATOM_COL + own
                    out[d, pl.ds((batches + own) * held + k, 1), :] = solved[a : a + 1, :]

    return pl.pallas_call(
        body,
        out_shape=jax.ShapeDtypeStruct((devices, rows_out, radial), F32),
        in_specs=[SMEM, VMEM, HBM],
        out_specs=VMEM,
        scratch_shapes=[
            pltpu.VMEM((lines, devices, radial), F32),
            pltpu.VMEM((held, radial, radial), F32),
            pltpu.SemaphoreType.DMA((held,)),
        ],
        compiler_params=params(53.5),
        name="radial_solve",
    )(degree_ids, arrived, green)


def potential_pass(active, slots, poles, rho, basis_t, harmonics, weights, shells, slot_count, blk, held):
    batches, span, points = basis_t.shape
    blocks = span // blk
    rows = harmonics.shape[1]
    devices, lines, radial = poles.shape
    wide = 2 * blk if blocks % 2 == 0 else blk

    def body(act, slot_ids, got, rho_hbm, phi_hbm, harm_hbm, wts, shell, out,
             phi, harm, rho, scaled, poles_keep, phi_sems, harm_sems, rho_sems):
        phi_loads = loads_of(phi_hbm, phi, phi_sems)
        harm_loads = loads_of(harm_hbm, harm, harm_sems)
        rho_loads = loads_of(rho_hbm, rho, rho_sems)
        for load in rho_loads + harm_loads + phi_loads:
            load.start()

        out[...] = jnp.zeros_like(out)
        if held * devices < rows:
            poles_keep[...] = jnp.zeros_like(poles_keep)
        for b in range(batches):
            for k in range(held):
                for d in range(devices):
                    line = d * held + k
                    if line < rows:
                        poles_keep[b, pl.ds(line, 1), :] = got[d, pl.ds(b * held + k, 1), :]

        factors = []
        for b in range(batches):
            rho_loads[b].wait()
            harm_loads[b].wait()
            ids = lax.broadcasted_iota(jnp.int32, (radial, points), 0)
            onehot = jnp.where(shell[b] == ids, 1.0, 0.0).astype(BF16)
            at_points = join2(
                jnp.dot(split2(poles_keep[b]), onehot, preferred_element_type=F32)
            )
            hartree = jnp.sum(harm[b] * at_points, axis=0, keepdims=True)
            root = jnp.exp(jnp.log(1.0 + rho[b] * rho[b]) * (-1.0 / 3.0))
            factors.append(wts[b] * (hartree - rho[b] * root))

        for b in range(batches):
            phi_loads[b].wait()
            scaled[b] = (phi[b].astype(F32) * factors[b]).astype(BF16)

        for b in range(batches):
            count = act[b]
            for first in range(0, span, wide):
                piece = lax.dot_general(
                    phi[b], scaled[b, pl.ds(first, wide), :], NT, preferred_element_type=F32
                )
                for i in range(blocks):
                    for j in range(first // blk, (first + wide) // blk):
                        live = (i < count) & (j < count)
                        slot = jnp.clip(slot_ids[b, i * blocks + j], 0, slot_count - 1)
                        left = j * blk - first
                        tile = piece[i * blk : (i + 1) * blk, left : left + blk].astype(BF16)
                        out[slot] = jnp.where(live, tile, out[slot])

    return pl.pallas_call(
        body,
        out_shape=jax.ShapeDtypeStruct((slot_count, blk, blk), BF16),
        in_specs=[SMEM, SMEM, VMEM, HBM, HBM, HBM, VMEM, VMEM],
        out_specs=VMEM,
        scratch_shapes=[
            pltpu.VMEM(basis_t.shape, BF16),
            pltpu.VMEM((batches, rows, points), F32),
            pltpu.VMEM((batches, 1, points), F32),
            pltpu.VMEM(basis_t.shape, BF16),
            pltpu.VMEM((batches, rows, radial), F32),
            pltpu.SemaphoreType.DMA((batches,)),
            pltpu.SemaphoreType.DMA((batches,)),
            pltpu.SemaphoreType.DMA((batches,)),
        ],
        compiler_params=params(62),
        name="potential_pass",
    )(active, slots, poles, rho, basis_t, harmonics, weights, shells)


def exchange(parts):
    return lax.all_to_all(parts, AXES, split_axis=0, concat_axis=0, tiled=True)


def shards(
    density_tiles,
    send_list,
    basis_values,
    active_blocks,
    touch_slots,
    point_weights,
    harmonics,
    shell_index,
    batch_atom,
    radial_green,
):
    devices = lax.axis_size(AXES)
    cols_count = lax.axis_size("col")
    capacity = send_list.shape[2]
    tiles_dev, blk, _ = density_tiles.shape
    batches, points, span = basis_values.shape
    harm_count = harmonics.shape[1]
    radial = radial_green.shape[1]
    slot_count = devices * capacity
    natoms = ATOM_COL * cols_count
    held = -(-harm_count // devices)
    rows = -(-harm_count // 16) * 16

    tile_ids = jnp.transpose(send_list, (2, 0, 1))
    outgoing = gather_tiles(tile_ids, density_tiles)
    arrived = exchange(outgoing.reshape(devices, capacity, blk, blk))
    received = arrived.reshape(slot_count, blk, blk)

    basis_t = jnp.transpose(basis_values, (0, 2, 1))
    harm_rows = jnp.pad(harmonics, ((0, 2 * batches), (0, rows - harm_count), (0, 0)))
    weights = point_weights[:, None, :]
    shells = shell_index[:, None, :]
    slots = touch_slots.reshape(batches, -1)

    rho, mom_out = density_pass(
        active_blocks, slots, batch_atom, received, basis_t, harm_rows, weights, shells,
        (held, radial), devices,
    )
    mom_in = exchange(mom_out)
    first = lax.axis_index(AXES) * held
    degree_ids = degrees(jnp.minimum(first + jnp.arange(held), harm_count - 1))
    poles_out = radial_solve(
        degree_ids, mom_in, radial_green, natoms, held, batches, cols_count
    )
    poles = exchange(poles_out)
    returning = potential_pass(
        active_blocks, slots, poles, rho, basis_t, harm_rows, weights, shells,
        slot_count, blk, held,
    )
    back = exchange(returning.reshape(devices, capacity, blk, blk))
    ham_tiles = sum_tiles(tile_ids, back.reshape(slot_count, blk, blk), tiles_dev)

    own = poles[:, batches * held :, :].reshape(devices, ATOM_COL, held, radial)
    own = jnp.transpose(own, (1, 0, 2, 3)).reshape(ATOM_COL, devices * held, radial)
    return (ham_tiles, own[:, :harm_count])


def solution(mesh):
    in_specs = (
        P(AXES, None, None),
        P(AXES, None, None),
        P(AXES, None, None),
        P(AXES),
        P(AXES, None, None),
        P(AXES, None),
        P(AXES, None, None),
        P(AXES, None),
        P(AXES),
        P(),
    )
    out_specs = (P(AXES, None, None), P("col", None, None))
    return jax.shard_map(shards, mesh=mesh, in_specs=in_specs, out_specs=out_specs, check_vma=False)
```

```python
import jax
import jax.numpy as jnp
from jax import lax
from jax.experimental import pallas as pl
from jax.experimental.pallas import tpu as pltpu
from jax.sharding import PartitionSpec as P

LDEG = 7
ATOM_COL = 2
AXES = ("row", "col")
F32 = jnp.float32
BF16 = jnp.bfloat16
NT = (((1,), (1,)), ((), ()))
SPARE = 256


def degrees(harm_ids):
    bounds = jnp.arange(1, LDEG) ** 2
    return jnp.sum((harm_ids[:, None] >= bounds[None, :]).astype(jnp.int32), axis=1)


SMEM = pl.BlockSpec(memory_space=pltpu.SMEM)
VMEM = pl.BlockSpec(memory_space=pltpu.VMEM)
HBM = pl.BlockSpec(memory_space=pltpu.HBM)


def params(mib):
    return pltpu.CompilerParams(vmem_limit_bytes=int(mib * 1024 * 1024))


def split2(values):
    high = values.astype(BF16)
    low = (values - high.astype(F32)).astype(BF16)
    return jnp.concatenate([high, low], axis=0)


def join2(stacked):
    rows = stacked.shape[0] // 2
    return stacked[:rows] + stacked[rows:]


def loads_of(source, held, sems):
    return [
        pltpu.make_async_copy(source.at[b], held.at[b], sems.at[b])
        for b in range(sems.shape[0])
    ]


def plan_views(plan, blocks):
    pairs = blocks * blocks
    return (
        lambda b: plan[b, pairs],
        lambda b, pair: plan[b, pair],
        lambda b: plan[b, pairs + 1],
    )


def gather_tiles(tile_ids, tiles):
    capacity, _, devices = tile_ids.shape
    count = capacity * devices

    def body(ids_hbm, tiles_ref, out_ref, keep, ids, sems):
        loads = [
            pltpu.make_async_copy(ids_hbm, ids, sems.at[2]),
            pltpu.make_async_copy(tiles_ref, keep, sems.at[0]),
        ]
        for load in loads:
            load.start()
        for load in loads:
            load.wait()

        def send(dev, carry):
            for k in range(capacity):
                pltpu.make_async_copy(
                    keep.at[ids[k, 0, dev]], out_ref.at[dev * capacity + k], sems.at[1]
                ).start()
            return carry

        lax.fori_loop(0, devices, send, 0, unroll=4)
        pltpu.make_async_copy(out_ref, out_ref, sems.at[1]).wait()

    return pl.pallas_call(
        body,
        out_shape=jax.ShapeDtypeStruct((count,) + tiles.shape[1:], tiles.dtype),
        in_specs=[HBM, HBM],
        out_specs=HBM,
        scratch_shapes=[
            pltpu.VMEM(tiles.shape, tiles.dtype),
            pltpu.SMEM(tile_ids.shape, jnp.int32),
            pltpu.SemaphoreType.DMA((3,)),
        ],
        compiler_params=params(63),
        name="gather_tiles",
    )(tile_ids, tiles)


def sum_tiles(tile_ids, arrived, tiles_dev):
    capacity, _, devices = tile_ids.shape
    _, blk, _ = arrived.shape

    def body(ids_hbm, arrived_ref, out_ref, ids, sem):
        load = pltpu.make_async_copy(ids_hbm, ids, sem)
        load.start()
        out_ref[...] = jnp.zeros_like(out_ref)
        load.wait()

        def add(dev, carry):
            for k in range(capacity):
                tile = ids[k, 0, dev]
                out_ref[tile] = out_ref[tile] + arrived_ref[dev * capacity + k].astype(F32)
            return carry

        lax.fori_loop(0, devices, add, 0, unroll=4)

    return pl.pallas_call(
        body,
        out_shape=jax.ShapeDtypeStruct((tiles_dev, blk, blk), F32),
        in_specs=[HBM, VMEM],
        out_specs=VMEM,
        scratch_shapes=[pltpu.SMEM(tile_ids.shape, jnp.int32), pltpu.SemaphoreType.DMA],
        compiler_params=params(16),
        name="sum_tiles",
    )(tile_ids, arrived)


def density_pass(plan, received, basis_t, harmonics, weights, shells, share, devices):
    batches, span, points = basis_t.shape
    slot_count, blk, _ = received.shape
    blocks = span // blk
    rows = harmonics.shape[1]
    held, radial = share
    lines = (held + 1) * batches

    def body(plan_hbm, recv, phi_hbm, harm_hbm, wts_hbm, shell_hbm, rho_hbm, send,
             phi, harm, rho, matrix, mom_keep, plan_keep, wts, shell,
             phi_sems, harm_sems, rho_sems, sems):
        phi_loads = loads_of(phi_hbm, phi, phi_sems)
        harm_loads = loads_of(harm_hbm, harm, harm_sems)
        rho_stores = loads_of(rho, rho_hbm, rho_sems)
        plan_load = pltpu.make_async_copy(plan_hbm, plan_keep, sems.at[0])
        point_loads = [
            pltpu.make_async_copy(wts_hbm, wts, sems.at[1]),
            pltpu.make_async_copy(shell_hbm, shell, sems.at[2]),
        ]
        for load in [plan_load] + phi_loads[:1] + point_loads + phi_loads[1:] + harm_loads:
            load.start()
        act, slot_ids, atom_ids = plan_views(plan_keep, blocks)
        plan_load.wait()

        for b in range(batches):
            count = act(b)
            for i in range(blocks):
                for j in range(blocks):
                    spot = (b, pl.ds(i * blk, blk), pl.ds(j * blk, blk))
                    live = (i < count) & (j < count)

                    @pl.when(live)
                    def _(b=b, i=i, j=j, spot=spot):
                        slot = jnp.clip(slot_ids(b, i * blocks + j), 0, slot_count - 1)
                        matrix[spot] = recv[slot]

                    @pl.when(jnp.logical_not(live))
                    def _(spot=spot):
                        matrix[spot] = jnp.zeros((blk, blk), BF16)

        for b in range(batches):
            send[:, pl.ds(held * batches + b, 1), :] = jnp.full(
                (devices, 1, radial), atom_ids(b).astype(F32), F32
            )

        def moments(b):
            weighted = harm[b] * (wts[b] * rho[b])
            ids = lax.broadcasted_iota(jnp.int32, (radial, points), 0)
            onehot = jnp.where(shell[b] == ids, 1.0, 0.0).astype(BF16)
            mom_keep[b] = join2(
                lax.dot_general(split2(weighted), onehot, NT, preferred_element_type=F32)
            )
            for k in range(held):
                for d in range(devices):
                    line = d * held + k
                    if line < rows:
                        send[d, pl.ds(k * batches + b, 1), :] = mom_keep[b, pl.ds(line, 1), :]
                    else:
                        send[d, pl.ds(k * batches + b, 1), :] = jnp.zeros((1, radial), F32)

        for b in range(batches):
            phi_loads[b].wait()
            product = jnp.dot(matrix[b], phi[b], preferred_element_type=F32)
            rho[b] = jnp.sum(product * phi[b].astype(F32), axis=0, keepdims=True)
            rho_stores[b].start()

        for load in point_loads:
            load.wait()
        for b in range(batches):
            harm_loads[b].wait()
            moments(b)
        for store in rho_stores:
            store.wait()

    return pl.pallas_call(
        body,
        out_shape=(
            jax.ShapeDtypeStruct((SPARE * batches, 1, points), F32),
            jax.ShapeDtypeStruct((devices, lines, radial), F32),
        ),
        in_specs=[HBM, VMEM, HBM, HBM, HBM, HBM],
        out_specs=(HBM, VMEM),
        scratch_shapes=[
            pltpu.VMEM(basis_t.shape, BF16),
            pltpu.VMEM((batches, rows, points), F32),
            pltpu.VMEM((batches, 1, points), F32),
            pltpu.VMEM((batches, span, span), BF16),
            pltpu.VMEM((batches, rows, radial), F32),
            pltpu.SMEM(plan.shape, jnp.int32),
            pltpu.VMEM((batches, 1, points), F32),
            pltpu.VMEM((batches, 1, points), jnp.int32),
            pltpu.SemaphoreType.DMA((batches,)),
            pltpu.SemaphoreType.DMA((batches,)),
            pltpu.SemaphoreType.DMA((batches,)),
            pltpu.SemaphoreType.DMA((3,)),
        ],
        compiler_params=params(52 - received.size * 2 / 2**20),
        name="density_pass",
    )(plan, received, basis_t, harmonics, weights, shells)


def radial_solve(degree_ids, arrived, green, natoms, held, batches, cols_count):
    devices, lines, radial = arrived.shape
    rows_out = (batches + ATOM_COL) * held

    def body(deg, got, green_hbm, out, flat, green, sems):
        loads = [
            pltpu.make_async_copy(green_hbm.at[deg[k]], green.at[k], sems.at[k])
            for k in range(held)
        ]
        for load in loads:
            load.start()
        for r in range(lines):
            for d in range(devices):
                flat[r, pl.ds(d, 1), :] = got[d, pl.ds(r, 1), :]
        atom_of = [flat[held * batches + b] for b in range(batches)]
        for k in range(held):
            sums = []
            for a in range(natoms):
                total = jnp.zeros((devices, radial), F32)
                for b in range(batches):
                    total = total + jnp.where(atom_of[b] == float(a), flat[k * batches + b], 0.0)
                sums.append(jnp.sum(total, axis=0, keepdims=True))
            atom_mom = jnp.concatenate(sums, axis=0)
            loads[k].wait()
            solved = lax.dot_general(
                atom_mom,
                green[k],
                NT,
                precision=lax.Precision.HIGHEST,
                preferred_element_type=F32,
            )
            for b in range(batches):
                picked = jnp.zeros((devices, radial), F32)
                for a in range(natoms):
                    picked = jnp.where(atom_of[b] == float(a), solved[a : a + 1, :], picked)
                for d in range(devices):
                    out[d, pl.ds(b * held + k, 1), :] = picked[d : d + 1, :]
            for own in range(ATOM_COL):
                for d in range(devices):
                    a = (d % cols_count) * ATOM_COL + own
                    out[d, pl.ds((batches + own) * held + k, 1), :] = solved[a : a + 1, :]

    return pl.pallas_call(
        body,
        out_shape=jax.ShapeDtypeStruct((devices, rows_out, radial), F32),
        in_specs=[SMEM, VMEM, HBM],
        out_specs=VMEM,
        scratch_shapes=[
            pltpu.VMEM((lines, devices, radial), F32),
            pltpu.VMEM((held, radial, radial), F32),
            pltpu.SemaphoreType.DMA((held,)),
        ],
        compiler_params=params(53.5),
        name="radial_solve",
    )(degree_ids, arrived, green)


def potential_pass(plan, poles, rho, basis_t, harmonics, weights, shells, slot_count, blk, held):
    batches, span, points = basis_t.shape
    blocks = span // blk
    rows = harmonics.shape[1]
    devices, lines, radial = poles.shape
    wide = 2 * blk if blocks % 2 == 0 else blk

    def body(plan_hbm, got, rho_hbm, phi_hbm, harm_hbm, wts_hbm, shell_hbm, out,
             phi, harm, rho, scaled, poles_keep, plan_keep, wts, shell,
             phi_sems, harm_sems, rho_sems, sems):
        phi_loads = loads_of(phi_hbm, phi, phi_sems)
        harm_loads = loads_of(harm_hbm, harm, harm_sems)
        rho_loads = loads_of(rho_hbm, rho, rho_sems)
        point_loads = [
            pltpu.make_async_copy(plan_hbm, plan_keep, sems.at[0]),
            pltpu.make_async_copy(wts_hbm, wts, sems.at[1]),
            pltpu.make_async_copy(shell_hbm, shell, sems.at[2]),
        ]
        for load in rho_loads + point_loads + harm_loads + phi_loads:
            load.start()
        act, slot_ids, _ = plan_views(plan_keep, blocks)

        out[...] = jnp.zeros_like(out)
        if held * devices < rows:
            poles_keep[...] = jnp.zeros_like(poles_keep)
        for b in range(batches):
            for k in range(held):
                for d in range(devices):
                    line = d * held + k
                    if line < rows:
                        poles_keep[b, pl.ds(line, 1), :] = got[d, pl.ds(b * held + k, 1), :]

        for load in point_loads:
            load.wait()
        factors = []
        for b in range(batches):
            rho_loads[b].wait()
            harm_loads[b].wait()
            ids = lax.broadcasted_iota(jnp.int32, (radial, points), 0)
            onehot = jnp.where(shell[b] == ids, 1.0, 0.0).astype(BF16)
            at_points = join2(
                jnp.dot(split2(poles_keep[b]), onehot, preferred_element_type=F32)
            )
            hartree = jnp.sum(harm[b] * at_points, axis=0, keepdims=True)
            root = jnp.exp(jnp.log(1.0 + rho[b] * rho[b]) * (-1.0 / 3.0))
            factors.append(wts[b] * (hartree - rho[b] * root))

        for load in phi_loads:
            load.wait()
        for b in range(batches):
            scaled[b] = (phi[b].astype(F32) * factors[b]).astype(BF16)
            count = act(b)
            for first in range(0, span, wide):
                piece = lax.dot_general(
                    phi[b], scaled[b, pl.ds(first, wide), :], NT, preferred_element_type=F32
                )
                for i in range(blocks):
                    for j in range(first // blk, (first + wide) // blk):
                        live = (i < count) & (j < count)
                        slot = jnp.clip(slot_ids(b, i * blocks + j), 0, slot_count - 1)
                        left = j * blk - first
                        tile = piece[i * blk : (i + 1) * blk, left : left + blk].astype(BF16)
                        out[slot] = jnp.where(live, tile, out[slot])

    return pl.pallas_call(
        body,
        out_shape=jax.ShapeDtypeStruct((slot_count, blk, blk), BF16),
        in_specs=[HBM, VMEM, HBM, HBM, HBM, HBM, HBM],
        out_specs=VMEM,
        scratch_shapes=[
            pltpu.VMEM(basis_t.shape, BF16),
            pltpu.VMEM((batches, rows, points), F32),
            pltpu.VMEM((batches, 1, points), F32),
            pltpu.VMEM(basis_t.shape, BF16),
            pltpu.VMEM((batches, rows, radial), F32),
            pltpu.SMEM(plan.shape, jnp.int32),
            pltpu.VMEM((batches, 1, points), F32),
            pltpu.VMEM((batches, 1, points), jnp.int32),
            pltpu.SemaphoreType.DMA((batches,)),
            pltpu.SemaphoreType.DMA((batches,)),
            pltpu.SemaphoreType.DMA((batches,)),
            pltpu.SemaphoreType.DMA((3,)),
        ],
        compiler_params=params(62),
        name="potential_pass",
    )(plan, poles, rho, basis_t, harmonics, weights, shells)


def exchange(parts):
    return lax.all_to_all(parts, AXES, split_axis=0, concat_axis=0, tiled=True)


def shards(
    density_tiles,
    send_list,
    basis_values,
    active_blocks,
    touch_slots,
    point_weights,
    harmonics,
    shell_index,
    batch_atom,
    radial_green,
):
    devices = lax.axis_size(AXES)
    cols_count = lax.axis_size("col")
    capacity = send_list.shape[2]
    tiles_dev, blk, _ = density_tiles.shape
    batches, points, span = basis_values.shape
    harm_count = harmonics.shape[1]
    radial = radial_green.shape[1]
    slot_count = devices * capacity
    natoms = ATOM_COL * cols_count
    held = -(-harm_count // devices)
    rows = -(-harm_count // 16) * 16

    tile_ids = jnp.transpose(send_list, (2, 0, 1))
    outgoing = gather_tiles(tile_ids, density_tiles)
    arrived = exchange(outgoing.reshape(devices, capacity, blk, blk))
    received = arrived.reshape(slot_count, blk, blk)

    basis_t = jnp.transpose(basis_values, (0, 2, 1))
    harm_rows = jnp.pad(harmonics, ((0, 2 * batches), (0, rows - harm_count), (0, 0)))
    weights = point_weights[:, None, :]
    shells = shell_index[:, None, :]
    plan = jnp.concatenate(
        [touch_slots.reshape(batches, -1), active_blocks[:, None], batch_atom[:, None]], axis=1
    )

    rho, mom_out = density_pass(
        plan, received, basis_t, harm_rows, weights, shells,
        (held, radial), devices,
    )
    mom_in = exchange(mom_out)
    first = lax.axis_index(AXES) * held
    degree_ids = degrees(jnp.minimum(first + jnp.arange(held), harm_count - 1))
    poles_out = radial_solve(
        degree_ids, mom_in, radial_green, natoms, held, batches, cols_count
    )
    poles = exchange(poles_out)
    returning = potential_pass(
        plan, poles, rho, basis_t, harm_rows, weights, shells,
        slot_count, blk, held,
    )
    back = exchange(returning.reshape(devices, capacity, blk, blk))
    ham_tiles = sum_tiles(tile_ids, back.reshape(slot_count, blk, blk), tiles_dev)

    own = poles[:, batches * held :, :].reshape(devices, ATOM_COL, held, radial)
    own = jnp.transpose(own, (1, 0, 2, 3)).reshape(ATOM_COL, devices * held, radial)
    return (ham_tiles, own[:, :harm_count])


def solution(mesh):
    in_specs = (
        P(AXES, None, None),
        P(AXES, None, None),
        P(AXES, None, None),
        P(AXES),
        P(AXES, None, None),
        P(AXES, None),
        P(AXES, None, None),
        P(AXES, None),
        P(AXES),
        P(),
    )
    out_specs = (P(AXES, None, None), P("col", None, None))
    return jax.shard_map(shards, mesh=mesh, in_specs=in_specs, out_specs=out_specs, check_vma=False)
```

```python
import jax
import jax.numpy as jnp
from jax import lax
from jax.experimental import pallas as pl
from jax.experimental.pallas import tpu as pltpu
from jax.sharding import PartitionSpec as P

LDEG = 7
ATOM_COL = 2
AXES = ("row", "col")
F32 = jnp.float32
BF16 = jnp.bfloat16
NT = (((1,), (1,)), ((), ()))
SPARE = 256


def degrees(harm_ids):
    bounds = jnp.arange(1, LDEG) ** 2
    return jnp.sum((harm_ids[:, None] >= bounds[None, :]).astype(jnp.int32), axis=1)


SMEM = pl.BlockSpec(memory_space=pltpu.SMEM)
VMEM = pl.BlockSpec(memory_space=pltpu.VMEM)
HBM = pl.BlockSpec(memory_space=pltpu.HBM)


def params(mib):
    return pltpu.CompilerParams(vmem_limit_bytes=int(mib * 1024 * 1024))


def split2(values):
    high = values.astype(BF16)
    low = (values - high.astype(F32)).astype(BF16)
    return jnp.concatenate([high, low], axis=0)


def join2(stacked):
    rows = stacked.shape[0] // 2
    return stacked[:rows] + stacked[rows:]


def loads_of(source, held, sems):
    return [
        pltpu.make_async_copy(source.at[b], held.at[b], sems.at[b])
        for b in range(sems.shape[0])
    ]


def plan_views(plan, blocks):
    pairs = blocks * blocks
    return (
        lambda b: plan[b, pairs],
        lambda b, pair: plan[b, pair],
        lambda b: plan[b, pairs + 1],
    )


def gather_tiles(tile_ids, tiles):
    capacity, _, devices = tile_ids.shape
    count = capacity * devices

    def body(ids_hbm, tiles_ref, out_ref, keep, ids, sems):
        loads = [
            pltpu.make_async_copy(ids_hbm, ids, sems.at[2]),
            pltpu.make_async_copy(tiles_ref, keep, sems.at[0]),
        ]
        for load in loads:
            load.start()
        for load in loads:
            load.wait()

        def send(dev, carry):
            for k in range(capacity):
                pltpu.make_async_copy(
                    keep.at[ids[k, 0, dev]], out_ref.at[dev * capacity + k], sems.at[1]
                ).start()
            return carry

        lax.fori_loop(0, devices, send, 0, unroll=4)
        pltpu.make_async_copy(out_ref, out_ref, sems.at[1]).wait()

    return pl.pallas_call(
        body,
        out_shape=jax.ShapeDtypeStruct((count,) + tiles.shape[1:], tiles.dtype),
        in_specs=[HBM, HBM],
        out_specs=HBM,
        scratch_shapes=[
            pltpu.VMEM(tiles.shape, tiles.dtype),
            pltpu.SMEM(tile_ids.shape, jnp.int32),
            pltpu.SemaphoreType.DMA((3,)),
        ],
        compiler_params=params(63),
        name="gather_tiles",
    )(tile_ids, tiles)


def sum_tiles(tile_ids, arrived, tiles_dev):
    capacity, _, devices = tile_ids.shape
    _, blk, _ = arrived.shape

    def body(ids_hbm, arrived_ref, out_ref, ids, sem):
        load = pltpu.make_async_copy(ids_hbm, ids, sem)
        load.start()
        out_ref[...] = jnp.zeros_like(out_ref)
        load.wait()

        def add(dev, carry):
            for k in range(capacity):
                tile = ids[k, 0, dev]
                out_ref[tile] = out_ref[tile] + arrived_ref[dev * capacity + k].astype(F32)
            return carry

        lax.fori_loop(0, devices, add, 0, unroll=4)

    return pl.pallas_call(
        body,
        out_shape=jax.ShapeDtypeStruct((tiles_dev, blk, blk), F32),
        in_specs=[HBM, VMEM],
        out_specs=VMEM,
        scratch_shapes=[pltpu.SMEM(tile_ids.shape, jnp.int32), pltpu.SemaphoreType.DMA],
        compiler_params=params(16),
        name="sum_tiles",
    )(tile_ids, arrived)


def density_pass(plan, received, basis_t, harmonics, weights, shells, share, devices):
    batches, span, points = basis_t.shape
    slot_count, blk, _ = received.shape
    blocks = span // blk
    rows = harmonics.shape[1]
    held, radial = share
    lines = (held + 1) * batches

    def body(plan_hbm, recv, phi_hbm, harm_hbm, wts_hbm, shell_hbm, rho_hbm, send,
             phi, harm, rho, matrix, mom_keep, plan_keep, wts, shell,
             phi_sems, harm_sems, rho_sems, sems):
        phi_loads = loads_of(phi_hbm, phi, phi_sems)
        harm_loads = loads_of(harm_hbm, harm, harm_sems)
        rho_stores = loads_of(rho, rho_hbm, rho_sems)
        plan_load = pltpu.make_async_copy(plan_hbm, plan_keep, sems.at[0])
        point_loads = [
            pltpu.make_async_copy(wts_hbm, wts, sems.at[1]),
            pltpu.make_async_copy(shell_hbm, shell, sems.at[2]),
        ]
        for load in [plan_load] + phi_loads[:1] + point_loads + phi_loads[1:] + harm_loads:
            load.start()
        act, slot_ids, atom_ids = plan_views(plan_keep, blocks)
        plan_load.wait()

        for b in range(batches):
            count = act(b)
            for i in range(blocks):
                for j in range(blocks):
                    spot = (b, pl.ds(i * blk, blk), pl.ds(j * blk, blk))
                    live = (i < count) & (j < count)

                    @pl.when(live)
                    def _(b=b, i=i, j=j, spot=spot):
                        slot = jnp.clip(slot_ids(b, i * blocks + j), 0, slot_count - 1)
                        matrix[spot] = recv[slot]

                    @pl.when(jnp.logical_not(live))
                    def _(spot=spot):
                        matrix[spot] = jnp.zeros((blk, blk), BF16)

        for b in range(batches):
            send[:, pl.ds(held * batches + b, 1), :] = jnp.full(
                (devices, 1, radial), atom_ids(b).astype(F32), F32
            )

        def moments(b):
            weighted = harm[b] * (wts[b] * rho[b])
            ids = lax.broadcasted_iota(jnp.int32, (radial, points), 0)
            onehot = jnp.where(shell[b] == ids, 1.0, 0.0).astype(BF16)
            mom_keep[b] = join2(
                lax.dot_general(split2(weighted), onehot, NT, preferred_element_type=F32)
            )
            for k in range(held):
                for d in range(devices):
                    line = d * held + k
                    if line < rows:
                        send[d, pl.ds(k * batches + b, 1), :] = mom_keep[b, pl.ds(line, 1), :]
                    else:
                        send[d, pl.ds(k * batches + b, 1), :] = jnp.zeros((1, radial), F32)

        for b in range(batches):
            phi_loads[b].wait()
            product = jnp.dot(matrix[b], phi[b], preferred_element_type=F32)
            rho[b] = jnp.sum(product * phi[b].astype(F32), axis=0, keepdims=True)
            rho_stores[b].start()

        for load in point_loads:
            load.wait()
        for b in range(batches):
            harm_loads[b].wait()
            moments(b)
        for store in rho_stores:
            store.wait()

    return pl.pallas_call(
        body,
        out_shape=(
            jax.ShapeDtypeStruct((SPARE * batches, 1, points), F32),
            jax.ShapeDtypeStruct((devices, lines, radial), F32),
        ),
        in_specs=[HBM, VMEM, HBM, HBM, HBM, HBM],
        out_specs=(HBM, VMEM),
        scratch_shapes=[
            pltpu.VMEM(basis_t.shape, BF16),
            pltpu.VMEM((batches, rows, points), F32),
            pltpu.VMEM((batches, 1, points), F32),
            pltpu.VMEM((batches, span, span), BF16),
            pltpu.VMEM((batches, rows, radial), F32),
            pltpu.SMEM(plan.shape, jnp.int32),
            pltpu.VMEM((batches, 1, points), F32),
            pltpu.VMEM((batches, 1, points), jnp.int32),
            pltpu.SemaphoreType.DMA((batches,)),
            pltpu.SemaphoreType.DMA((batches,)),
            pltpu.SemaphoreType.DMA((batches,)),
            pltpu.SemaphoreType.DMA((3,)),
        ],
        compiler_params=params(52 - received.size * 2 / 2**20),
        name="density_pass",
    )(plan, received, basis_t, harmonics, weights, shells)


def radial_solve(arrived, green, natoms, held, batches, cols_count):
    devices, lines, radial = arrived.shape
    rows_out = (batches + ATOM_COL) * held

    def body(got, green_hbm, out, flat, green, sems):
        loads = [
            pltpu.make_async_copy(green_hbm.at[k], green.at[k], sems.at[k]) for k in range(held)
        ]
        for load in loads:
            load.start()
        for r in range(lines):
            for d in range(devices):
                flat[r, pl.ds(d, 1), :] = got[d, pl.ds(r, 1), :]
        atom_of = [flat[held * batches + b] for b in range(batches)]
        for k in range(held):
            sums = []
            for a in range(natoms):
                total = jnp.zeros((devices, radial), F32)
                for b in range(batches):
                    total = total + jnp.where(atom_of[b] == float(a), flat[k * batches + b], 0.0)
                sums.append(jnp.sum(total, axis=0, keepdims=True))
            atom_mom = jnp.concatenate(sums, axis=0)
            loads[k].wait()
            solved = lax.dot_general(
                atom_mom,
                green[k],
                NT,
                precision=lax.Precision.HIGHEST,
                preferred_element_type=F32,
            )
            for b in range(batches):
                picked = jnp.zeros((devices, radial), F32)
                for a in range(natoms):
                    picked = jnp.where(atom_of[b] == float(a), solved[a : a + 1, :], picked)
                for d in range(devices):
                    out[d, pl.ds(b * held + k, 1), :] = picked[d : d + 1, :]
            for own in range(ATOM_COL):
                for d in range(devices):
                    a = (d % cols_count) * ATOM_COL + own
                    out[d, pl.ds((batches + own) * held + k, 1), :] = solved[a : a + 1, :]

    return pl.pallas_call(
        body,
        out_shape=jax.ShapeDtypeStruct((devices, rows_out, radial), F32),
        in_specs=[VMEM, HBM],
        out_specs=VMEM,
        scratch_shapes=[
            pltpu.VMEM((lines, devices, radial), F32),
            pltpu.VMEM((held, radial, radial), F32),
            pltpu.SemaphoreType.DMA((held,)),
        ],
        compiler_params=params(53.5),
        name="radial_solve",
    )(arrived, green)


def potential_pass(plan, poles, rho, basis_t, harmonics, weights, shells, slot_count, blk, held):
    batches, span, points = basis_t.shape
    blocks = span // blk
    rows = harmonics.shape[1]
    devices, lines, radial = poles.shape
    wide = 2 * blk if blocks % 2 == 0 else blk

    def body(plan_hbm, got, rho_hbm, phi_hbm, harm_hbm, wts_hbm, shell_hbm, out,
             phi, harm, rho, scaled, poles_keep, plan_keep, wts, shell,
             phi_sems, harm_sems, rho_sems, sems):
        phi_loads = loads_of(phi_hbm, phi, phi_sems)
        harm_loads = loads_of(harm_hbm, harm, harm_sems)
        rho_loads = loads_of(rho_hbm, rho, rho_sems)
        point_loads = [
            pltpu.make_async_copy(plan_hbm, plan_keep, sems.at[0]),
            pltpu.make_async_copy(wts_hbm, wts, sems.at[1]),
            pltpu.make_async_copy(shell_hbm, shell, sems.at[2]),
        ]
        for load in rho_loads + point_loads + harm_loads + phi_loads:
            load.start()
        act, slot_ids, _ = plan_views(plan_keep, blocks)

        out[...] = jnp.zeros_like(out)
        if held * devices < rows:
            poles_keep[...] = jnp.zeros_like(poles_keep)
        for b in range(batches):
            for k in range(held):
                for d in range(devices):
                    line = d * held + k
                    if line < rows:
                        poles_keep[b, pl.ds(line, 1), :] = got[d, pl.ds(b * held + k, 1), :]

        for load in point_loads:
            load.wait()
        factors = []
        for b in range(batches):
            rho_loads[b].wait()
            harm_loads[b].wait()
            ids = lax.broadcasted_iota(jnp.int32, (radial, points), 0)
            onehot = jnp.where(shell[b] == ids, 1.0, 0.0).astype(BF16)
            at_points = join2(
                jnp.dot(split2(poles_keep[b]), onehot, preferred_element_type=F32)
            )
            hartree = jnp.sum(harm[b] * at_points, axis=0, keepdims=True)
            root = jnp.exp(jnp.log(1.0 + rho[b] * rho[b]) * (-1.0 / 3.0))
            factors.append(wts[b] * (hartree - rho[b] * root))

        def keep(b, i, j, tile):
            live = (i < act(b)) & (j < act(b))
            slot = jnp.clip(slot_ids(b, i * blocks + j), 0, slot_count - 1)
            out[slot] = jnp.where(live, tile, out[slot])

        for load in phi_loads:
            load.wait()
        for b in range(batches):
            scaled[b] = (phi[b].astype(F32) * factors[b]).astype(BF16)
            for first in range(0, span, wide):
                piece = lax.dot_general(
                    phi[b, pl.ds(first, span - first), :],
                    scaled[b, pl.ds(first, wide), :],
                    NT,
                    preferred_element_type=F32,
                )
                for i in range(first // blk, blocks):
                    for j in range(first // blk, (first + wide) // blk):
                        top, left = i * blk - first, j * blk - first
                        tile = piece[top : top + blk, left : left + blk].astype(BF16)
                        keep(b, i, j, tile)
                        if i * blk >= first + wide:
                            keep(b, j, i, tile.T)

    return pl.pallas_call(
        body,
        out_shape=jax.ShapeDtypeStruct((slot_count, blk, blk), BF16),
        in_specs=[HBM, VMEM, HBM, HBM, HBM, HBM, HBM],
        out_specs=VMEM,
        scratch_shapes=[
            pltpu.VMEM(basis_t.shape, BF16),
            pltpu.VMEM((batches, rows, points), F32),
            pltpu.VMEM((batches, 1, points), F32),
            pltpu.VMEM(basis_t.shape, BF16),
            pltpu.VMEM((batches, rows, radial), F32),
            pltpu.SMEM(plan.shape, jnp.int32),
            pltpu.VMEM((batches, 1, points), F32),
            pltpu.VMEM((batches, 1, points), jnp.int32),
            pltpu.SemaphoreType.DMA((batches,)),
            pltpu.SemaphoreType.DMA((batches,)),
            pltpu.SemaphoreType.DMA((batches,)),
            pltpu.SemaphoreType.DMA((3,)),
        ],
        compiler_params=params(62),
        name="potential_pass",
    )(plan, poles, rho, basis_t, harmonics, weights, shells)


def exchange(parts):
    return lax.all_to_all(parts, AXES, split_axis=0, concat_axis=0, tiled=True)


def shards(
    density_tiles,
    send_list,
    basis_values,
    active_blocks,
    touch_slots,
    point_weights,
    harmonics,
    shell_index,
    batch_atom,
    radial_green,
):
    devices = lax.axis_size(AXES)
    cols_count = lax.axis_size("col")
    capacity = send_list.shape[2]
    tiles_dev, blk, _ = density_tiles.shape
    batches, points, span = basis_values.shape
    harm_count = harmonics.shape[1]
    radial = radial_green.shape[1]
    slot_count = devices * capacity
    natoms = ATOM_COL * cols_count
    held = -(-harm_count // devices)
    rows = -(-harm_count // 16) * 16

    tile_ids = jnp.transpose(send_list, (2, 0, 1))
    outgoing = gather_tiles(tile_ids, density_tiles)
    arrived = exchange(outgoing.reshape(devices, capacity, blk, blk))
    received = arrived.reshape(slot_count, blk, blk)

    basis_t = jnp.transpose(basis_values, (0, 2, 1))
    harm_rows = jnp.pad(harmonics, ((0, 2 * batches), (0, rows - harm_count), (0, 0)))
    weights = point_weights[:, None, :]
    shells = shell_index[:, None, :]
    plan = jnp.concatenate(
        [touch_slots.reshape(batches, -1), active_blocks[:, None], batch_atom[:, None]], axis=1
    )

    rho, mom_out = density_pass(
        plan, received, basis_t, harm_rows, weights, shells,
        (held, radial), devices,
    )
    mom_in = exchange(mom_out)
    first = lax.axis_index(AXES) * held
    degree_ids = degrees(jnp.minimum(first + jnp.arange(held), harm_count - 1))
    green_own = jnp.concatenate(
        [lax.dynamic_slice_in_dim(radial_green, degree_ids[k], 1) for k in range(held)]
    )
    poles_out = radial_solve(
        mom_in, green_own, natoms, held, batches, cols_count
    )
    poles = exchange(poles_out)
    returning = potential_pass(
        plan, poles, rho, basis_t, harm_rows, weights, shells,
        slot_count, blk, held,
    )
    back = exchange(returning.reshape(devices, capacity, blk, blk))
    ham_tiles = sum_tiles(tile_ids, back.reshape(slot_count, blk, blk), tiles_dev)

    own = poles[:, batches * held :, :].reshape(devices, ATOM_COL, held, radial)
    own = jnp.transpose(own, (1, 0, 2, 3)).reshape(ATOM_COL, devices * held, radial)
    return (ham_tiles, own[:, :harm_count])


def solution(mesh):
    in_specs = (
        P(AXES, None, None),
        P(AXES, None, None),
        P(AXES, None, None),
        P(AXES),
        P(AXES, None, None),
        P(AXES, None),
        P(AXES, None, None),
        P(AXES, None),
        P(AXES),
        P(),
    )
    out_specs = (P(AXES, None, None), P("col", None, None))
    return jax.shard_map(shards, mesh=mesh, in_specs=in_specs, out_specs=out_specs, check_vma=False)
```

```python
import jax
import jax.numpy as jnp
from jax import lax
from jax.experimental import pallas as pl
from jax.experimental.pallas import tpu as pltpu
from jax.sharding import PartitionSpec as P

LDEG = 7
ATOM_COL = 2
AXES = ("row", "col")
F32 = jnp.float32
BF16 = jnp.bfloat16
NT = (((1,), (1,)), ((), ()))
SPARE = 256


def degrees(harm_ids):
    bounds = jnp.arange(1, LDEG) ** 2
    return jnp.sum((harm_ids[:, None] >= bounds[None, :]).astype(jnp.int32), axis=1)


SMEM = pl.BlockSpec(memory_space=pltpu.SMEM)
VMEM = pl.BlockSpec(memory_space=pltpu.VMEM)
HBM = pl.BlockSpec(memory_space=pltpu.HBM)


def params(mib):
    return pltpu.CompilerParams(vmem_limit_bytes=int(mib * 1024 * 1024))


def split2(values):
    high = values.astype(BF16)
    low = (values - high.astype(F32)).astype(BF16)
    return jnp.concatenate([high, low], axis=0)


def join2(stacked):
    rows = stacked.shape[0] // 2
    return stacked[:rows] + stacked[rows:]


def loads_of(source, held, sems):
    return [
        pltpu.make_async_copy(source.at[b], held.at[b], sems.at[b])
        for b in range(sems.shape[0])
    ]


def plan_views(plan, blocks):
    pairs = blocks * blocks
    return lambda b: plan[b, pairs], lambda b, pair: plan[b, pair]


def gather_tiles(tile_ids, tiles):
    capacity, _, devices = tile_ids.shape
    count = capacity * devices

    def body(ids_hbm, tiles_ref, out_ref, keep, ids, sems):
        loads = [
            pltpu.make_async_copy(ids_hbm, ids, sems.at[2]),
            pltpu.make_async_copy(tiles_ref, keep, sems.at[0]),
        ]
        for load in loads:
            load.start()
        for load in loads:
            load.wait()

        def send(dev, carry):
            for k in range(capacity):
                pltpu.make_async_copy(
                    keep.at[ids[k, 0, dev]], out_ref.at[dev * capacity + k], sems.at[1]
                ).start()
            return carry

        lax.fori_loop(0, devices, send, 0, unroll=4)
        pltpu.make_async_copy(out_ref, out_ref, sems.at[1]).wait()

    return pl.pallas_call(
        body,
        out_shape=jax.ShapeDtypeStruct((count,) + tiles.shape[1:], tiles.dtype),
        in_specs=[HBM, HBM],
        out_specs=HBM,
        scratch_shapes=[
            pltpu.VMEM(tiles.shape, tiles.dtype),
            pltpu.SMEM(tile_ids.shape, jnp.int32),
            pltpu.SemaphoreType.DMA((3,)),
        ],
        compiler_params=params(63),
        name="gather_tiles",
    )(tile_ids, tiles)


def sum_tiles(tile_ids, arrived, tiles_dev):
    capacity, _, devices = tile_ids.shape
    _, blk, _ = arrived.shape

    def body(ids_hbm, arrived_ref, out_ref, ids, sem):
        load = pltpu.make_async_copy(ids_hbm, ids, sem)
        load.start()
        out_ref[...] = jnp.zeros_like(out_ref)
        load.wait()

        def add(dev, carry):
            for k in range(capacity):
                tile = ids[k, 0, dev]
                out_ref[tile] = out_ref[tile] + arrived_ref[dev * capacity + k].astype(F32)
            return carry

        lax.fori_loop(0, devices, add, 0, unroll=4)

    return pl.pallas_call(
        body,
        out_shape=jax.ShapeDtypeStruct((tiles_dev, blk, blk), F32),
        in_specs=[HBM, VMEM],
        out_specs=VMEM,
        scratch_shapes=[pltpu.SMEM(tile_ids.shape, jnp.int32), pltpu.SemaphoreType.DMA],
        compiler_params=params(16),
        name="sum_tiles",
    )(tile_ids, arrived)


def density_pass(plan, received, basis_t, harmonics, weights, shells, share, devices):
    batches, span, points = basis_t.shape
    slot_count, blk, _ = received.shape
    blocks = span // blk
    rows = harmonics.shape[1]
    held, radial = share
    lines = held * batches

    def body(plan_hbm, recv, phi_hbm, harm_hbm, wts_hbm, shell_hbm, rho_hbm, send,
             phi, harm, rho, matrix, mom_keep, plan_keep, wts, shell,
             phi_sems, harm_sems, rho_sems, sems):
        phi_loads = loads_of(phi_hbm, phi, phi_sems)
        harm_loads = loads_of(harm_hbm, harm, harm_sems)
        rho_stores = loads_of(rho, rho_hbm, rho_sems)
        plan_load = pltpu.make_async_copy(plan_hbm, plan_keep, sems.at[0])
        point_loads = [
            pltpu.make_async_copy(wts_hbm, wts, sems.at[1]),
            pltpu.make_async_copy(shell_hbm, shell, sems.at[2]),
        ]
        for load in [plan_load] + phi_loads[:1] + point_loads + phi_loads[1:] + harm_loads:
            load.start()
        act, slot_ids = plan_views(plan_keep, blocks)
        plan_load.wait()

        for b in range(batches):
            count = act(b)
            for i in range(blocks):
                for j in range(blocks):
                    spot = (b, pl.ds(i * blk, blk), pl.ds(j * blk, blk))
                    live = (i < count) & (j < count)

                    @pl.when(live)
                    def _(b=b, i=i, j=j, spot=spot):
                        slot = jnp.clip(slot_ids(b, i * blocks + j), 0, slot_count - 1)
                        matrix[spot] = recv[slot]

                    @pl.when(jnp.logical_not(live))
                    def _(spot=spot):
                        matrix[spot] = jnp.zeros((blk, blk), BF16)

        def moments(b):
            weighted = harm[b] * (wts[b] * rho[b])
            ids = lax.broadcasted_iota(jnp.int32, (radial, points), 0)
            onehot = jnp.where(shell[b] == ids, 1.0, 0.0).astype(BF16)
            mom_keep[b] = join2(
                lax.dot_general(split2(weighted), onehot, NT, preferred_element_type=F32)
            )
            for k in range(held):
                for d in range(devices):
                    line = d * held + k
                    if line < rows:
                        send[d, pl.ds(k * batches + b, 1), :] = mom_keep[b, pl.ds(line, 1), :]
                    else:
                        send[d, pl.ds(k * batches + b, 1), :] = jnp.zeros((1, radial), F32)

        for b in range(batches):
            phi_loads[b].wait()
            product = jnp.dot(matrix[b], phi[b], preferred_element_type=F32)
            rho[b] = jnp.sum(product * phi[b].astype(F32), axis=0, keepdims=True)
            rho_stores[b].start()

        for load in point_loads + harm_loads:
            load.wait()
        for b in range(batches):
            moments(b)
        for store in rho_stores:
            store.wait()

    return pl.pallas_call(
        body,
        out_shape=(
            jax.ShapeDtypeStruct((SPARE * batches, 1, points), F32),
            jax.ShapeDtypeStruct((devices, lines, radial), F32),
        ),
        in_specs=[HBM, VMEM, HBM, HBM, HBM, HBM],
        out_specs=(HBM, VMEM),
        scratch_shapes=[
            pltpu.VMEM(basis_t.shape, BF16),
            pltpu.VMEM((batches, rows, points), F32),
            pltpu.VMEM((batches, 1, points), F32),
            pltpu.VMEM((batches, span, span), BF16),
            pltpu.VMEM((batches, rows, radial), F32),
            pltpu.SMEM(plan.shape, jnp.int32),
            pltpu.VMEM((batches, 1, points), F32),
            pltpu.VMEM((batches, 1, points), jnp.int32),
            pltpu.SemaphoreType.DMA((batches,)),
            pltpu.SemaphoreType.DMA((batches,)),
            pltpu.SemaphoreType.DMA((batches,)),
            pltpu.SemaphoreType.DMA((3,)),
        ],
        compiler_params=params(52 - received.size * 2 / 2**20),
        name="density_pass",
    )(plan, received, basis_t, harmonics, weights, shells)


def radial_solve(arrived, green, atoms, natoms, held, batches, cols_count):
    devices, lines, radial = arrived.shape
    rows_out = (batches + ATOM_COL) * held

    def body(got, green_hbm, atom_ref, out, flat, green, sems):
        loads = [
            pltpu.make_async_copy(green_hbm.at[k], green.at[k], sems.at[k]) for k in range(held)
        ]
        for load in loads:
            load.start()
        for r in range(lines):
            for d in range(devices):
                flat[r, pl.ds(d, 1), :] = got[d, pl.ds(r, 1), :]
        atom_of = [atom_ref[b] for b in range(batches)]
        for k in range(held):
            sums = []
            for a in range(natoms):
                total = jnp.zeros((devices, radial), F32)
                for b in range(batches):
                    total = total + jnp.where(atom_of[b] == a, flat[k * batches + b], 0.0)
                sums.append(jnp.sum(total, axis=0, keepdims=True))
            atom_mom = jnp.concatenate(sums, axis=0)
            loads[k].wait()
            solved = lax.dot_general(
                atom_mom,
                green[k],
                NT,
                precision=lax.Precision.HIGHEST,
                preferred_element_type=F32,
            )
            for b in range(batches):
                picked = jnp.zeros((devices, radial), F32)
                for a in range(natoms):
                    picked = jnp.where(atom_of[b] == a, solved[a : a + 1, :], picked)
                for d in range(devices):
                    out[d, pl.ds(b * held + k, 1), :] = picked[d : d + 1, :]
            for own in range(ATOM_COL):
                for d in range(devices):
                    a = (d % cols_count) * ATOM_COL + own
                    out[d, pl.ds((batches + own) * held + k, 1), :] = solved[a : a + 1, :]

    return pl.pallas_call(
        body,
        out_shape=jax.ShapeDtypeStruct((devices, rows_out, radial), F32),
        in_specs=[VMEM, HBM, VMEM],
        out_specs=VMEM,
        scratch_shapes=[
            pltpu.VMEM((lines, devices, radial), F32),
            pltpu.VMEM((held, radial, radial), F32),
            pltpu.SemaphoreType.DMA((held,)),
        ],
        compiler_params=params(53.5),
        name="radial_solve",
    )(arrived, green, atoms)


def potential_pass(plan, poles, rho, basis_t, harmonics, weights, shells, slot_count, blk, held):
    batches, span, points = basis_t.shape
    blocks = span // blk
    rows = harmonics.shape[1]
    devices, lines, radial = poles.shape
    wide = 2 * blk if blocks % 2 == 0 else blk

    def body(plan_hbm, got, rho_hbm, phi_hbm, harm_hbm, wts_hbm, shell_hbm, out,
             phi, harm, rho, scaled, poles_keep, plan_keep, wts, shell,
             phi_sems, harm_sems, rho_sems, sems):
        phi_loads = loads_of(phi_hbm, phi, phi_sems)
        harm_loads = loads_of(harm_hbm, harm, harm_sems)
        rho_loads = loads_of(rho_hbm, rho, rho_sems)
        point_loads = [
            pltpu.make_async_copy(plan_hbm, plan_keep, sems.at[0]),
            pltpu.make_async_copy(wts_hbm, wts, sems.at[1]),
            pltpu.make_async_copy(shell_hbm, shell, sems.at[2]),
        ]
        for load in rho_loads + point_loads + harm_loads + phi_loads:
            load.start()
        act, slot_ids = plan_views(plan_keep, blocks)

        out[...] = jnp.zeros_like(out)
        if held * devices < rows:
            poles_keep[...] = jnp.zeros_like(poles_keep)
        for b in range(batches):
            for k in range(held):
                for d in range(devices):
                    line = d * held + k
                    if line < rows:
                        poles_keep[b, pl.ds(line, 1), :] = got[d, pl.ds(b * held + k, 1), :]

        for load in point_loads:
            load.wait()
        factors = []
        for b in range(batches):
            rho_loads[b].wait()
            harm_loads[b].wait()
            ids = lax.broadcasted_iota(jnp.int32, (radial, points), 0)
            onehot = jnp.where(shell[b] == ids, 1.0, 0.0).astype(BF16)
            at_points = join2(
                jnp.dot(split2(poles_keep[b]), onehot, preferred_element_type=F32)
            )
            hartree = jnp.sum(harm[b] * at_points, axis=0, keepdims=True)
            root = jnp.exp(jnp.log(1.0 + rho[b] * rho[b]) * (-1.0 / 3.0))
            factors.append(wts[b] * (hartree - rho[b] * root))

        def keep(b, i, j, tile):
            live = (i < act(b)) & (j < act(b))
            slot = jnp.clip(slot_ids(b, i * blocks + j), 0, slot_count - 1)
            out[slot] = jnp.where(live, tile, out[slot])

        for load in phi_loads:
            load.wait()
        for b in range(batches):
            scaled[b] = (phi[b].astype(F32) * factors[b]).astype(BF16)
            for first in range(0, span, wide):
                piece = lax.dot_general(
                    phi[b, pl.ds(first, span - first), :],
                    scaled[b, pl.ds(first, wide), :],
                    NT,
                    preferred_element_type=F32,
                )
                for i in range(first // blk, blocks):
                    for j in range(first // blk, (first + wide) // blk):
                        top, left = i * blk - first, j * blk - first
                        tile = piece[top : top + blk, left : left + blk].astype(BF16)
                        keep(b, i, j, tile)
                        if i * blk >= first + wide:
                            keep(b, j, i, tile.T)

    return pl.pallas_call(
        body,
        out_shape=jax.ShapeDtypeStruct((slot_count, blk, blk), BF16),
        in_specs=[HBM, VMEM, HBM, HBM, HBM, HBM, HBM],
        out_specs=VMEM,
        scratch_shapes=[
            pltpu.VMEM(basis_t.shape, BF16),
            pltpu.VMEM((batches, rows, points), F32),
            pltpu.VMEM((batches, 1, points), F32),
            pltpu.VMEM(basis_t.shape, BF16),
            pltpu.VMEM((batches, rows, radial), F32),
            pltpu.SMEM(plan.shape, jnp.int32),
            pltpu.VMEM((batches, 1, points), F32),
            pltpu.VMEM((batches, 1, points), jnp.int32),
            pltpu.SemaphoreType.DMA((batches,)),
            pltpu.SemaphoreType.DMA((batches,)),
            pltpu.SemaphoreType.DMA((batches,)),
            pltpu.SemaphoreType.DMA((3,)),
        ],
        compiler_params=params(62),
        name="potential_pass",
    )(plan, poles, rho, basis_t, harmonics, weights, shells)


def gathered(values, devices):
    me = lax.axis_index(AXES)
    reach = 1
    while reach < devices:
        other = lax.ppermute(values, AXES, [(d, d ^ reach) for d in range(devices)])
        upper = (me & reach) > 0
        low, high = jnp.where(upper, other, values), jnp.where(upper, values, other)
        values = jnp.concatenate([low, high])
        reach *= 2
    return values


def exchange(parts):
    return lax.all_to_all(parts, AXES, split_axis=0, concat_axis=0, tiled=True)


def shards(
    density_tiles,
    send_list,
    basis_values,
    active_blocks,
    touch_slots,
    point_weights,
    harmonics,
    shell_index,
    batch_atom,
    radial_green,
):
    devices = lax.axis_size(AXES)
    cols_count = lax.axis_size("col")
    capacity = send_list.shape[2]
    tiles_dev, blk, _ = density_tiles.shape
    batches, points, span = basis_values.shape
    harm_count = harmonics.shape[1]
    radial = radial_green.shape[1]
    slot_count = devices * capacity
    natoms = ATOM_COL * cols_count
    held = -(-harm_count // devices)
    rows = -(-harm_count // 16) * 16

    tile_ids = jnp.transpose(send_list, (2, 0, 1))
    outgoing = gather_tiles(tile_ids, density_tiles)
    outgoing, own_atoms = lax.optimization_barrier((outgoing, batch_atom))
    arrived = exchange(outgoing.reshape(devices, capacity, blk, blk))
    all_atoms = gathered(own_atoms, devices).reshape(devices, batches)
    atom_rows = jnp.broadcast_to(all_atoms.T[:, :, None], (batches, devices, radial))
    received = arrived.reshape(slot_count, blk, blk)

    basis_t = jnp.transpose(basis_values, (0, 2, 1))
    harm_rows = jnp.pad(harmonics, ((0, 2 * batches), (0, rows - harm_count), (0, 0)))
    weights = point_weights[:, None, :]
    shells = shell_index[:, None, :]
    plan = jnp.concatenate(
        [touch_slots.reshape(batches, -1), active_blocks[:, None]], axis=1
    )

    rho, mom_out = density_pass(
        plan, received, basis_t, harm_rows, weights, shells,
        (held, radial), devices,
    )
    mom_in = exchange(mom_out)
    first = lax.axis_index(AXES) * held
    degree_ids = degrees(jnp.minimum(first + jnp.arange(held), harm_count - 1))
    green_own = jnp.concatenate(
        [lax.dynamic_slice_in_dim(radial_green, degree_ids[k], 1) for k in range(held)]
    )
    poles_out = radial_solve(
        mom_in, green_own, atom_rows, natoms, held, batches, cols_count
    )
    poles = exchange(poles_out)
    returning = potential_pass(
        plan, poles, rho, basis_t, harm_rows, weights, shells,
        slot_count, blk, held,
    )
    back = exchange(returning.reshape(devices, capacity, blk, blk))
    ham_tiles = sum_tiles(tile_ids, back.reshape(slot_count, blk, blk), tiles_dev)

    own = poles[:, batches * held :, :].reshape(devices, ATOM_COL, held, radial)
    own = jnp.transpose(own, (1, 0, 2, 3)).reshape(ATOM_COL, devices * held, radial)
    return (ham_tiles, own[:, :harm_count])


def solution(mesh):
    in_specs = (
        P(AXES, None, None),
        P(AXES, None, None),
        P(AXES, None, None),
        P(AXES),
        P(AXES, None, None),
        P(AXES, None),
        P(AXES, None, None),
        P(AXES, None),
        P(AXES),
        P(),
    )
    out_specs = (P(AXES, None, None), P("col", None, None))
    return jax.shard_map(shards, mesh=mesh, in_specs=in_specs, out_specs=out_specs, check_vma=False)
```

```python
import jax
import jax.numpy as jnp
from jax import lax
from jax.experimental import pallas as pl
from jax.experimental.pallas import tpu as pltpu
from jax.sharding import PartitionSpec as P

LDEG = 7
ATOM_COL = 2
AXES = ("row", "col")
F32 = jnp.float32
BF16 = jnp.bfloat16
NT = (((1,), (1,)), ((), ()))
SPARE = 256


def degrees(harm_ids):
    bounds = jnp.arange(1, LDEG) ** 2
    return jnp.sum((harm_ids[:, None] >= bounds[None, :]).astype(jnp.int32), axis=1)


SMEM = pl.BlockSpec(memory_space=pltpu.SMEM)
VMEM = pl.BlockSpec(memory_space=pltpu.VMEM)
HBM = pl.BlockSpec(memory_space=pltpu.HBM)


def params(mib):
    return pltpu.CompilerParams(vmem_limit_bytes=int(mib * 1024 * 1024))


def split2(values):
    high = values.astype(BF16)
    low = (values - high.astype(F32)).astype(BF16)
    return jnp.concatenate([high, low], axis=0)


def join2(stacked):
    rows = stacked.shape[0] // 2
    return stacked[:rows] + stacked[rows:]


def loads_of(source, held, sems):
    return [
        pltpu.make_async_copy(source.at[b], held.at[b], sems.at[b])
        for b in range(sems.shape[0])
    ]


def plan_views(plan, blocks):
    pairs = blocks * blocks
    return lambda b: plan[b, pairs], lambda b, pair: plan[b, pair]


def gather_tiles(tile_ids, tiles):
    capacity, _, devices = tile_ids.shape
    count = capacity * devices

    def body(ids_hbm, tiles_ref, out_ref, keep, ids, sems):
        loads = [
            pltpu.make_async_copy(ids_hbm, ids, sems.at[2]),
            pltpu.make_async_copy(tiles_ref, keep, sems.at[0]),
        ]
        for load in loads:
            load.start()
        for load in loads:
            load.wait()

        def send(dev, carry):
            for k in range(capacity):
                pltpu.make_async_copy(
                    keep.at[ids[k, 0, dev]], out_ref.at[dev * capacity + k], sems.at[1]
                ).start()
            return carry

        lax.fori_loop(0, devices, send, 0, unroll=4)
        pltpu.make_async_copy(out_ref, out_ref, sems.at[1]).wait()

    return pl.pallas_call(
        body,
        out_shape=jax.ShapeDtypeStruct((count,) + tiles.shape[1:], tiles.dtype),
        in_specs=[HBM, HBM],
        out_specs=HBM,
        scratch_shapes=[
            pltpu.VMEM(tiles.shape, tiles.dtype),
            pltpu.SMEM(tile_ids.shape, jnp.int32),
            pltpu.SemaphoreType.DMA((3,)),
        ],
        compiler_params=params(63),
        name="gather_tiles",
    )(tile_ids, tiles)


def sum_tiles(tile_ids, arrived, tiles_dev):
    capacity, _, devices = tile_ids.shape
    _, blk, _ = arrived.shape

    def body(ids_hbm, arrived_ref, out_ref, ids, sem):
        load = pltpu.make_async_copy(ids_hbm, ids, sem)
        load.start()
        out_ref[...] = jnp.zeros_like(out_ref)
        load.wait()

        def add(dev, carry):
            for k in range(capacity):
                tile = ids[k, 0, dev]
                out_ref[tile] = out_ref[tile] + arrived_ref[dev * capacity + k].astype(F32)
            return carry

        lax.fori_loop(0, devices, add, 0, unroll=4)

    return pl.pallas_call(
        body,
        out_shape=jax.ShapeDtypeStruct((tiles_dev, blk, blk), F32),
        in_specs=[HBM, VMEM],
        out_specs=VMEM,
        scratch_shapes=[pltpu.SMEM(tile_ids.shape, jnp.int32), pltpu.SemaphoreType.DMA],
        compiler_params=params(16),
        name="sum_tiles",
    )(tile_ids, arrived)


def density_pass(plan, received, basis_t, harmonics, weights, shells, share, devices):
    batches, span, points = basis_t.shape
    slot_count, blk, _ = received.shape
    blocks = span // blk
    rows = harmonics.shape[1]
    held, radial = share
    lines = held * batches

    def body(plan_hbm, recv, phi_hbm, harm_hbm, wts_hbm, shell_hbm, rho_hbm, send,
             phi, harm, rho, matrix, mom_keep, plan_keep, wts, shell,
             phi_sems, harm_sems, rho_sems, sems):
        phi_loads = loads_of(phi_hbm, phi, phi_sems)
        harm_loads = loads_of(harm_hbm, harm, harm_sems)
        rho_stores = loads_of(rho, rho_hbm, rho_sems)
        plan_load = pltpu.make_async_copy(plan_hbm, plan_keep, sems.at[0])
        point_loads = [
            pltpu.make_async_copy(wts_hbm, wts, sems.at[1]),
            pltpu.make_async_copy(shell_hbm, shell, sems.at[2]),
        ]
        for load in [plan_load] + phi_loads[:1] + point_loads + phi_loads[1:] + harm_loads:
            load.start()
        act, slot_ids = plan_views(plan_keep, blocks)
        plan_load.wait()

        for b in range(batches):
            count = act(b)
            for i in range(blocks):
                for j in range(blocks):
                    spot = (b, pl.ds(i * blk, blk), pl.ds(j * blk, blk))
                    live = (i < count) & (j < count)

                    @pl.when(live)
                    def _(b=b, i=i, j=j, spot=spot):
                        slot = jnp.clip(slot_ids(b, i * blocks + j), 0, slot_count - 1)
                        matrix[spot] = recv[slot]

                    @pl.when(jnp.logical_not(live))
                    def _(spot=spot):
                        matrix[spot] = jnp.zeros((blk, blk), BF16)

        def moments(b):
            weighted = harm[b] * (wts[b] * rho[b])
            ids = lax.broadcasted_iota(jnp.int32, (radial, points), 0)
            onehot = jnp.where(shell[b] == ids, 1.0, 0.0).astype(BF16)
            mom_keep[b] = join2(
                lax.dot_general(split2(weighted), onehot, NT, preferred_element_type=F32)
            )
            for k in range(held):
                for d in range(devices):
                    line = d * held + k
                    if line < rows:
                        send[d, pl.ds(k * batches + b, 1), :] = mom_keep[b, pl.ds(line, 1), :]
                    else:
                        send[d, pl.ds(k * batches + b, 1), :] = jnp.zeros((1, radial), F32)

        for b in range(batches):
            phi_loads[b].wait()
            product = jnp.dot(matrix[b], phi[b], preferred_element_type=F32)
            rho[b] = jnp.sum(product * phi[b].astype(F32), axis=0, keepdims=True)
            rho_stores[b].start()

        for load in point_loads + harm_loads:
            load.wait()
        for b in range(batches):
            moments(b)
        for store in rho_stores:
            store.wait()

    return pl.pallas_call(
        body,
        out_shape=(
            jax.ShapeDtypeStruct((SPARE * batches, 1, points), F32),
            jax.ShapeDtypeStruct((devices, lines, radial), F32),
        ),
        in_specs=[HBM, VMEM, HBM, HBM, HBM, HBM],
        out_specs=(HBM, VMEM),
        scratch_shapes=[
            pltpu.VMEM(basis_t.shape, BF16),
            pltpu.VMEM((batches, rows, points), F32),
            pltpu.VMEM((batches, 1, points), F32),
            pltpu.VMEM((batches, span, span), BF16),
            pltpu.VMEM((batches, rows, radial), F32),
            pltpu.SMEM(plan.shape, jnp.int32),
            pltpu.VMEM((batches, 1, points), F32),
            pltpu.VMEM((batches, 1, points), jnp.int32),
            pltpu.SemaphoreType.DMA((batches,)),
            pltpu.SemaphoreType.DMA((batches,)),
            pltpu.SemaphoreType.DMA((batches,)),
            pltpu.SemaphoreType.DMA((3,)),
        ],
        compiler_params=params(52 - received.size * 2 / 2**20),
        name="density_pass",
    )(plan, received, basis_t, harmonics, weights, shells)


def radial_solve(arrived, green, atoms, natoms, held, batches, cols_count):
    devices, lines, radial = arrived.shape
    rows_out = (batches + ATOM_COL) * held

    def body(got, green_hbm, atom_ref, out, flat, green, sems):
        loads = [
            pltpu.make_async_copy(green_hbm.at[k], green.at[k], sems.at[k]) for k in range(held)
        ]
        for load in loads:
            load.start()
        for r in range(lines):
            for d in range(devices):
                flat[r, pl.ds(d, 1), :] = got[d, pl.ds(r, 1), :]
        atom_of = [atom_ref[b] for b in range(batches)]
        for k in range(held):
            sums = []
            for a in range(natoms):
                total = jnp.zeros((devices, radial), F32)
                for b in range(batches):
                    total = total + jnp.where(atom_of[b] == a, flat[k * batches + b], 0.0)
                sums.append(jnp.sum(total, axis=0, keepdims=True))
            atom_mom = jnp.concatenate(sums, axis=0)
            loads[k].wait()
            solved = lax.dot_general(
                atom_mom,
                green[k],
                NT,
                precision=lax.Precision.HIGHEST,
                preferred_element_type=F32,
            )
            for b in range(batches):
                picked = jnp.zeros((devices, radial), F32)
                for a in range(natoms):
                    picked = jnp.where(atom_of[b] == a, solved[a : a + 1, :], picked)
                for d in range(devices):
                    out[d, pl.ds(b * held + k, 1), :] = picked[d : d + 1, :]
            for own in range(ATOM_COL):
                for d in range(devices):
                    a = (d % cols_count) * ATOM_COL + own
                    out[d, pl.ds((batches + own) * held + k, 1), :] = solved[a : a + 1, :]

    return pl.pallas_call(
        body,
        out_shape=jax.ShapeDtypeStruct((devices, rows_out, radial), F32),
        in_specs=[VMEM, HBM, VMEM],
        out_specs=VMEM,
        scratch_shapes=[
            pltpu.VMEM((lines, devices, radial), F32),
            pltpu.VMEM((held, radial, radial), F32),
            pltpu.SemaphoreType.DMA((held,)),
        ],
        compiler_params=params(53.5),
        name="radial_solve",
    )(arrived, green, atoms)


def potential_pass(plan, poles, rho, basis_t, harmonics, weights, shells, slot_count, blk, held):
    batches, span, points = basis_t.shape
    blocks = span // blk
    rows = harmonics.shape[1]
    devices, lines, radial = poles.shape
    wide = 2 * blk if blocks % 2 == 0 else blk

    def body(plan_hbm, got, rho_hbm, phi_hbm, harm_hbm, wts_hbm, shell_hbm, out_hbm,
             out, last, last_sems, phi, harm, rho, scaled, poles_keep, plan_keep, wts, shell,
             phi_sems, harm_sems, rho_sems, sems):
        phi_loads = loads_of(phi_hbm, phi, phi_sems)
        harm_loads = loads_of(harm_hbm, harm, harm_sems)
        rho_loads = loads_of(rho_hbm, rho, rho_sems)
        point_loads = [
            pltpu.make_async_copy(plan_hbm, plan_keep, sems.at[0]),
            pltpu.make_async_copy(wts_hbm, wts, sems.at[1]),
            pltpu.make_async_copy(shell_hbm, shell, sems.at[2]),
        ]
        for load in rho_loads + point_loads + harm_loads + phi_loads:
            load.start()
        act, slot_ids = plan_views(plan_keep, blocks)

        out[...] = jnp.zeros_like(out)
        if held * devices < rows:
            poles_keep[...] = jnp.zeros_like(poles_keep)
        for b in range(batches):
            for k in range(held):
                for d in range(devices):
                    line = d * held + k
                    if line < rows:
                        poles_keep[b, pl.ds(line, 1), :] = got[d, pl.ds(b * held + k, 1), :]

        for load in point_loads:
            load.wait()
        factors = []
        for b in range(batches):
            rho_loads[b].wait()
            harm_loads[b].wait()
            ids = lax.broadcasted_iota(jnp.int32, (radial, points), 0)
            onehot = jnp.where(shell[b] == ids, 1.0, 0.0).astype(BF16)
            at_points = join2(
                jnp.dot(split2(poles_keep[b]), onehot, preferred_element_type=F32)
            )
            hartree = jnp.sum(harm[b] * at_points, axis=0, keepdims=True)
            root = jnp.exp(jnp.log(1.0 + rho[b] * rho[b]) * (-1.0 / 3.0))
            factors.append(wts[b] * (hartree - rho[b] * root))

        def keep(b, i, j, tile):
            live = (i < act(b)) & (j < act(b))
            slot = jnp.clip(slot_ids(b, i * blocks + j), 0, slot_count - 1)
            if b < batches - 1:
                out[slot] = jnp.where(live, tile, out[slot])
            else:
                last[i * blocks + j] = tile

        def last_tiles(act_on):
            for i in range(blocks):
                for j in range(blocks):
                    pair = i * blocks + j

                    @pl.when((i < act(batches - 1)) & (j < act(batches - 1)))
                    def _(pair=pair):
                        slot = jnp.clip(slot_ids(batches - 1, pair), 0, slot_count - 1)
                        act_on(
                            pltpu.make_async_copy(
                                last.at[pair], out_hbm.at[slot], last_sems.at[pair]
                            )
                        )

        bulk = pltpu.make_async_copy(out, out_hbm, sems.at[3])
        for load in phi_loads:
            load.wait()
        for b in range(batches):
            scaled[b] = (phi[b].astype(F32) * factors[b]).astype(BF16)
        for b in range(batches):
            if b == batches - 1:
                bulk.start()
            for first in range(0, span, wide):
                piece = lax.dot_general(
                    phi[b, pl.ds(first, span - first), :],
                    scaled[b, pl.ds(first, wide), :],
                    NT,
                    preferred_element_type=F32,
                )
                for i in range(first // blk, blocks):
                    for j in range(first // blk, (first + wide) // blk):
                        top, left = i * blk - first, j * blk - first
                        tile = piece[top : top + blk, left : left + blk].astype(BF16)
                        keep(b, i, j, tile)
                        if i * blk >= first + wide:
                            keep(b, j, i, tile.T)
        bulk.wait()
        last_tiles(lambda copy: copy.start())
        last_tiles(lambda copy: copy.wait())

    return pl.pallas_call(
        body,
        out_shape=jax.ShapeDtypeStruct((slot_count, blk, blk), BF16),
        in_specs=[HBM, VMEM, HBM, HBM, HBM, HBM, HBM],
        out_specs=HBM,
        scratch_shapes=[
            pltpu.VMEM((slot_count, blk, blk), BF16),
            pltpu.VMEM((blocks * blocks, blk, blk), BF16),
            pltpu.SemaphoreType.DMA((blocks * blocks,)),
            pltpu.VMEM(basis_t.shape, BF16),
            pltpu.VMEM((batches, rows, points), F32),
            pltpu.VMEM((batches, 1, points), F32),
            pltpu.VMEM(basis_t.shape, BF16),
            pltpu.VMEM((batches, rows, radial), F32),
            pltpu.SMEM(plan.shape, jnp.int32),
            pltpu.VMEM((batches, 1, points), F32),
            pltpu.VMEM((batches, 1, points), jnp.int32),
            pltpu.SemaphoreType.DMA((batches,)),
            pltpu.SemaphoreType.DMA((batches,)),
            pltpu.SemaphoreType.DMA((batches,)),
            pltpu.SemaphoreType.DMA((4,)),
        ],
        compiler_params=params(62),
        name="potential_pass",
    )(plan, poles, rho, basis_t, harmonics, weights, shells)


def gathered(values, devices):
    me = lax.axis_index(AXES)
    reach = 1
    while reach < devices:
        other = lax.ppermute(values, AXES, [(d, d ^ reach) for d in range(devices)])
        upper = (me & reach) > 0
        low, high = jnp.where(upper, other, values), jnp.where(upper, values, other)
        values = jnp.concatenate([low, high])
        reach *= 2
    return values


def exchange(parts):
    return lax.all_to_all(parts, AXES, split_axis=0, concat_axis=0, tiled=True)


def shards(
    density_tiles,
    send_list,
    basis_values,
    active_blocks,
    touch_slots,
    point_weights,
    harmonics,
    shell_index,
    batch_atom,
    radial_green,
):
    devices = lax.axis_size(AXES)
    cols_count = lax.axis_size("col")
    capacity = send_list.shape[2]
    tiles_dev, blk, _ = density_tiles.shape
    batches, points, span = basis_values.shape
    harm_count = harmonics.shape[1]
    radial = radial_green.shape[1]
    slot_count = devices * capacity
    natoms = ATOM_COL * cols_count
    held = -(-harm_count // devices)
    rows = -(-harm_count // 16) * 16

    tile_ids = jnp.transpose(send_list, (2, 0, 1))
    outgoing = gather_tiles(tile_ids, density_tiles)
    outgoing, own_atoms = lax.optimization_barrier((outgoing, batch_atom))
    arrived = exchange(outgoing.reshape(devices, capacity, blk, blk))
    all_atoms = gathered(own_atoms, devices).reshape(devices, batches)
    atom_rows = jnp.broadcast_to(all_atoms.T[:, :, None], (batches, devices, radial))
    received = arrived.reshape(slot_count, blk, blk)

    basis_t = jnp.transpose(basis_values, (0, 2, 1))
    harm_rows = jnp.pad(harmonics, ((0, 2 * batches), (0, rows - harm_count), (0, 0)))
    weights = point_weights[:, None, :]
    shells = shell_index[:, None, :]
    plan = jnp.concatenate(
        [touch_slots.reshape(batches, -1), active_blocks[:, None]], axis=1
    )

    rho, mom_out = density_pass(
        plan, received, basis_t, harm_rows, weights, shells,
        (held, radial), devices,
    )
    mom_in = exchange(mom_out)
    first = lax.axis_index(AXES) * held
    degree_ids = degrees(jnp.minimum(first + jnp.arange(held), harm_count - 1))
    green_own = jnp.concatenate(
        [lax.dynamic_slice_in_dim(radial_green, degree_ids[k], 1) for k in range(held)]
    )
    poles_out = radial_solve(
        mom_in, green_own, atom_rows, natoms, held, batches, cols_count
    )
    poles = exchange(poles_out)
    returning = potential_pass(
        plan, poles, rho, basis_t, harm_rows, weights, shells,
        slot_count, blk, held,
    )
    back = exchange(returning.reshape(devices, capacity, blk, blk))
    ham_tiles = sum_tiles(tile_ids, back.reshape(slot_count, blk, blk), tiles_dev)

    own = poles[:, batches * held :, :].reshape(devices, ATOM_COL, held, radial)
    own = jnp.transpose(own, (1, 0, 2, 3)).reshape(ATOM_COL, devices * held, radial)
    return (ham_tiles, own[:, :harm_count])


def solution(mesh):
    in_specs = (
        P(AXES, None, None),
        P(AXES, None, None),
        P(AXES, None, None),
        P(AXES),
        P(AXES, None, None),
        P(AXES, None),
        P(AXES, None, None),
        P(AXES, None),
        P(AXES),
        P(),
    )
    out_specs = (P(AXES, None, None), P("col", None, None))
    return jax.shard_map(shards, mesh=mesh, in_specs=in_specs, out_specs=out_specs, check_vma=False)
```

```python
import jax
import jax.numpy as jnp
from jax import lax
from jax.experimental import pallas as pl
from jax.experimental.pallas import tpu as pltpu
from jax.sharding import PartitionSpec as P

LDEG = 7
ATOM_COL = 2
AXES = ("row", "col")
F32 = jnp.float32
BF16 = jnp.bfloat16
NT = (((1,), (1,)), ((), ()))
SPARE = 256


def degrees(harm_ids):
    bounds = jnp.arange(1, LDEG) ** 2
    return jnp.sum((harm_ids[:, None] >= bounds[None, :]).astype(jnp.int32), axis=1)


SMEM = pl.BlockSpec(memory_space=pltpu.SMEM)
VMEM = pl.BlockSpec(memory_space=pltpu.VMEM)
HBM = pl.BlockSpec(memory_space=pltpu.HBM)


def params(mib):
    return pltpu.CompilerParams(vmem_limit_bytes=int(mib * 1024 * 1024))


def split2(values):
    high = values.astype(BF16)
    low = (values - high.astype(F32)).astype(BF16)
    return jnp.concatenate([high, low], axis=0)


def join2(stacked):
    rows = stacked.shape[0] // 2
    return stacked[:rows] + stacked[rows:]


def loads_of(source, held, sems):
    return [
        pltpu.make_async_copy(source.at[b], held.at[b], sems.at[b])
        for b in range(sems.shape[0])
    ]


def plan_views(plan, blocks):
    pairs = blocks * blocks
    return lambda b: plan[b, pairs], lambda b, pair: plan[b, pair]


def gather_tiles(tile_ids, tiles):
    capacity, _, devices = tile_ids.shape
    count = capacity * devices

    def body(ids_hbm, tiles_ref, out_ref, keep, ids, sems):
        loads = [
            pltpu.make_async_copy(ids_hbm, ids, sems.at[2]),
            pltpu.make_async_copy(tiles_ref, keep, sems.at[0]),
        ]
        for load in loads:
            load.start()
        for load in loads:
            load.wait()

        def send(dev, carry):
            for k in range(capacity):
                pltpu.make_async_copy(
                    keep.at[ids[k, 0, dev]], out_ref.at[dev * capacity + k], sems.at[1]
                ).start()
            return carry

        lax.fori_loop(0, devices, send, 0, unroll=4)
        pltpu.make_async_copy(out_ref, out_ref, sems.at[1]).wait()

    return pl.pallas_call(
        body,
        out_shape=jax.ShapeDtypeStruct((count,) + tiles.shape[1:], tiles.dtype),
        in_specs=[HBM, HBM],
        out_specs=HBM,
        scratch_shapes=[
            pltpu.VMEM(tiles.shape, tiles.dtype),
            pltpu.SMEM(tile_ids.shape, jnp.int32),
            pltpu.SemaphoreType.DMA((3,)),
        ],
        compiler_params=params(63),
        name="gather_tiles",
    )(tile_ids, tiles)


def sum_tiles(tile_ids, arrived, tiles_dev):
    capacity, _, devices = tile_ids.shape
    _, blk, _ = arrived.shape

    def body(ids_hbm, arrived_ref, out_ref, ids, sem):
        load = pltpu.make_async_copy(ids_hbm, ids, sem)
        load.start()
        out_ref[...] = jnp.zeros_like(out_ref)
        load.wait()

        def add(dev, carry):
            for k in range(capacity):
                tile = ids[k, 0, dev]
                out_ref[tile] = out_ref[tile] + arrived_ref[dev * capacity + k].astype(F32)
            return carry

        lax.fori_loop(0, devices, add, 0, unroll=4)

    return pl.pallas_call(
        body,
        out_shape=jax.ShapeDtypeStruct((tiles_dev, blk, blk), F32),
        in_specs=[HBM, VMEM],
        out_specs=VMEM,
        scratch_shapes=[pltpu.SMEM(tile_ids.shape, jnp.int32), pltpu.SemaphoreType.DMA],
        compiler_params=params(16),
        name="sum_tiles",
    )(tile_ids, arrived)


def density_pass(plan, received, basis_t, harmonics, weights, shells, share, devices):
    batches, span, points = basis_t.shape
    slot_count, blk, _ = received.shape
    blocks = span // blk
    rows = harmonics.shape[1]
    held, radial = share
    lines = held * batches

    def body(plan_hbm, recv, phi_hbm, harm_hbm, wts_hbm, shell_hbm, rho_hbm, send,
             phi, harm, rho, matrix, mom_keep, plan_keep, wts, shell,
             phi_sems, harm_sems, rho_sems, sems):
        phi_loads = loads_of(phi_hbm, phi, phi_sems)
        harm_loads = loads_of(harm_hbm, harm, harm_sems)
        rho_stores = loads_of(rho, rho_hbm, rho_sems)
        plan_load = pltpu.make_async_copy(plan_hbm, plan_keep, sems.at[0])
        point_loads = [
            pltpu.make_async_copy(wts_hbm, wts, sems.at[1]),
            pltpu.make_async_copy(shell_hbm, shell, sems.at[2]),
        ]
        for load in [plan_load] + phi_loads[:1] + point_loads + phi_loads[1:] + harm_loads:
            load.start()
        act, slot_ids = plan_views(plan_keep, blocks)
        plan_load.wait()

        for b in range(batches):
            count = act(b)
            for i in range(blocks):
                for j in range(blocks):
                    spot = (b, pl.ds(i * blk, blk), pl.ds(j * blk, blk))
                    live = (i < count) & (j < count)

                    @pl.when(live)
                    def _(b=b, i=i, j=j, spot=spot):
                        slot = jnp.clip(slot_ids(b, i * blocks + j), 0, slot_count - 1)
                        matrix[spot] = recv[slot]

                    @pl.when(jnp.logical_not(live))
                    def _(spot=spot):
                        matrix[spot] = jnp.zeros((blk, blk), BF16)

        def moments(b):
            weighted = harm[b] * (wts[b] * rho[b])
            ids = lax.broadcasted_iota(jnp.int32, (radial, points), 0)
            onehot = jnp.where(shell[b] == ids, 1.0, 0.0).astype(BF16)
            mom_keep[b] = join2(
                lax.dot_general(split2(weighted), onehot, NT, preferred_element_type=F32)
            )
            for k in range(held):
                for d in range(devices):
                    line = d * held + k
                    if line < rows:
                        send[d, pl.ds(k * batches + b, 1), :] = mom_keep[b, pl.ds(line, 1), :]
                    else:
                        send[d, pl.ds(k * batches + b, 1), :] = jnp.zeros((1, radial), F32)

        for b in range(batches):
            phi_loads[b].wait()
            product = jnp.dot(matrix[b], phi[b], preferred_element_type=F32)
            rho[b] = jnp.sum(product * phi[b].astype(F32), axis=0, keepdims=True)
            rho_stores[b].start()

        for load in point_loads + harm_loads:
            load.wait()
        for b in range(batches):
            moments(b)
        for store in rho_stores:
            store.wait()

    return pl.pallas_call(
        body,
        out_shape=(
            jax.ShapeDtypeStruct((SPARE * batches, 1, points), F32),
            jax.ShapeDtypeStruct((devices, lines, radial), F32),
        ),
        in_specs=[HBM, VMEM, HBM, HBM, HBM, HBM],
        out_specs=(HBM, VMEM),
        scratch_shapes=[
            pltpu.VMEM(basis_t.shape, BF16),
            pltpu.VMEM((batches, rows, points), F32),
            pltpu.VMEM((batches, 1, points), F32),
            pltpu.VMEM((batches, span, span), BF16),
            pltpu.VMEM((batches, rows, radial), F32),
            pltpu.SMEM(plan.shape, jnp.int32),
            pltpu.VMEM((batches, 1, points), F32),
            pltpu.VMEM((batches, 1, points), jnp.int32),
            pltpu.SemaphoreType.DMA((batches,)),
            pltpu.SemaphoreType.DMA((batches,)),
            pltpu.SemaphoreType.DMA((batches,)),
            pltpu.SemaphoreType.DMA((3,)),
        ],
        compiler_params=params(52 - received.size * 2 / 2**20),
        name="density_pass",
    )(plan, received, basis_t, harmonics, weights, shells)


def radial_solve(arrived, green, atoms, natoms, held, batches, cols_count):
    devices, lines, radial = arrived.shape
    rows_out = (batches + ATOM_COL) * held

    def body(got, green_hbm, atom_ref, out, flat, green, sems):
        loads = [
            pltpu.make_async_copy(green_hbm.at[k], green.at[k], sems.at[k]) for k in range(held)
        ]
        for load in loads:
            load.start()
        for r in range(lines):
            for d in range(devices):
                flat[r, pl.ds(d, 1), :] = got[d, pl.ds(r, 1), :]
        atom_of = [atom_ref[b] for b in range(batches)]
        for k in range(held):
            sums = []
            for a in range(natoms):
                total = jnp.zeros((devices, radial), F32)
                for b in range(batches):
                    total = total + jnp.where(atom_of[b] == a, flat[k * batches + b], 0.0)
                sums.append(jnp.sum(total, axis=0, keepdims=True))
            atom_mom = jnp.concatenate(sums, axis=0)
            loads[k].wait()
            solved = lax.dot_general(
                atom_mom,
                green[k],
                NT,
                precision=lax.Precision.HIGHEST,
                preferred_element_type=F32,
            )
            for b in range(batches):
                picked = jnp.zeros((devices, radial), F32)
                for a in range(natoms):
                    picked = jnp.where(atom_of[b] == a, solved[a : a + 1, :], picked)
                for d in range(devices):
                    out[d, pl.ds(b * held + k, 1), :] = picked[d : d + 1, :]
            for own in range(ATOM_COL):
                for d in range(devices):
                    a = (d % cols_count) * ATOM_COL + own
                    out[d, pl.ds((batches + own) * held + k, 1), :] = solved[a : a + 1, :]

    return pl.pallas_call(
        body,
        out_shape=jax.ShapeDtypeStruct((devices, rows_out, radial), F32),
        in_specs=[VMEM, HBM, VMEM],
        out_specs=VMEM,
        scratch_shapes=[
            pltpu.VMEM((lines, devices, radial), F32),
            pltpu.VMEM((held, radial, radial), F32),
            pltpu.SemaphoreType.DMA((held,)),
        ],
        compiler_params=params(53.5),
        name="radial_solve",
    )(arrived, green, atoms)


def potential_pass(plan, poles, rho, basis_t, harmonics, weights, shells, slot_count, blk, held):
    batches, span, points = basis_t.shape
    blocks = span // blk
    rows = harmonics.shape[1]
    devices, lines, radial = poles.shape
    wide = 2 * blk if blocks % 2 == 0 else blk

    def body(plan_hbm, got, rho_hbm, phi_hbm, harm_hbm, wts_hbm, shell_hbm, out_hbm,
             out, last, last_sems, phi, harm, rho, scaled, poles_keep, plan_keep, wts, shell,
             phi_sems, harm_sems, rho_sems, sems):
        phi_loads = loads_of(phi_hbm, phi, phi_sems)
        harm_loads = loads_of(harm_hbm, harm, harm_sems)
        rho_loads = loads_of(rho_hbm, rho, rho_sems)
        point_loads = [
            pltpu.make_async_copy(plan_hbm, plan_keep, sems.at[0]),
            pltpu.make_async_copy(wts_hbm, wts, sems.at[1]),
            pltpu.make_async_copy(shell_hbm, shell, sems.at[2]),
        ]
        for load in rho_loads + point_loads + harm_loads + phi_loads:
            load.start()
        act, slot_ids = plan_views(plan_keep, blocks)

        out[...] = jnp.zeros_like(out)
        if held * devices < rows:
            poles_keep[...] = jnp.zeros_like(poles_keep)
        for b in range(batches):
            for k in range(held):
                for d in range(devices):
                    line = d * held + k
                    if line < rows:
                        poles_keep[b, pl.ds(line, 1), :] = got[d, pl.ds(b * held + k, 1), :]

        for load in point_loads:
            load.wait()
        factors = []
        for b in range(batches):
            rho_loads[b].wait()
            harm_loads[b].wait()
            ids = lax.broadcasted_iota(jnp.int32, (radial, points), 0)
            onehot = jnp.where(shell[b] == ids, 1.0, 0.0).astype(BF16)
            at_points = join2(
                jnp.dot(split2(poles_keep[b]), onehot, preferred_element_type=F32)
            )
            hartree = jnp.sum(harm[b] * at_points, axis=0, keepdims=True)
            root = jnp.exp(jnp.log(1.0 + rho[b] * rho[b]) * (-1.0 / 3.0))
            factors.append(wts[b] * (hartree - rho[b] * root))

        def keep(b, i, j, tile):
            live = (i < act(b)) & (j < act(b))
            slot = jnp.clip(slot_ids(b, i * blocks + j), 0, slot_count - 1)
            if b < batches - 1:
                out[slot] = jnp.where(live, tile, out[slot])
            else:
                last[i * blocks + j] = tile

        def last_tiles(act_on):
            for i in range(blocks):
                for j in range(blocks):
                    pair = i * blocks + j

                    @pl.when((i < act(batches - 1)) & (j < act(batches - 1)))
                    def _(pair=pair):
                        slot = jnp.clip(slot_ids(batches - 1, pair), 0, slot_count - 1)
                        act_on(
                            pltpu.make_async_copy(
                                last.at[pair], out_hbm.at[slot], last_sems.at[pair]
                            )
                        )

        bulk = pltpu.make_async_copy(out, out_hbm, sems.at[3])
        for b in range(batches):
            phi_loads[b].wait()
            scaled[b] = (phi[b].astype(F32) * factors[b]).astype(BF16)
            if b == batches - 1:
                bulk.start()
            for first in range(0, span, wide):
                piece = lax.dot_general(
                    phi[b, pl.ds(first, span - first), :],
                    scaled[b, pl.ds(first, wide), :],
                    NT,
                    preferred_element_type=F32,
                )
                for i in range(first // blk, blocks):
                    for j in range(first // blk, (first + wide) // blk):
                        top, left = i * blk - first, j * blk - first
                        tile = piece[top : top + blk, left : left + blk].astype(BF16)
                        keep(b, i, j, tile)
                        if i * blk >= first + wide:
                            keep(b, j, i, tile.T)
        bulk.wait()
        last_tiles(lambda copy: copy.start())
        last_tiles(lambda copy: copy.wait())

    return pl.pallas_call(
        body,
        out_shape=jax.ShapeDtypeStruct((slot_count, blk, blk), BF16),
        in_specs=[HBM, VMEM, HBM, HBM, HBM, HBM, HBM],
        out_specs=HBM,
        scratch_shapes=[
            pltpu.VMEM((slot_count, blk, blk), BF16),
            pltpu.VMEM((blocks * blocks, blk, blk), BF16),
            pltpu.SemaphoreType.DMA((blocks * blocks,)),
            pltpu.VMEM(basis_t.shape, BF16),
            pltpu.VMEM((batches, rows, points), F32),
            pltpu.VMEM((batches, 1, points), F32),
            pltpu.VMEM(basis_t.shape, BF16),
            pltpu.VMEM((batches, rows, radial), F32),
            pltpu.SMEM(plan.shape, jnp.int32),
            pltpu.VMEM((batches, 1, points), F32),
            pltpu.VMEM((batches, 1, points), jnp.int32),
            pltpu.SemaphoreType.DMA((batches,)),
            pltpu.SemaphoreType.DMA((batches,)),
            pltpu.SemaphoreType.DMA((batches,)),
            pltpu.SemaphoreType.DMA((4,)),
        ],
        compiler_params=params(62),
        name="potential_pass",
    )(plan, poles, rho, basis_t, harmonics, weights, shells)


def gathered(values, devices):
    me = lax.axis_index(AXES)
    reach = 1
    while reach < devices:
        other = lax.ppermute(values, AXES, [(d, d ^ reach) for d in range(devices)])
        upper = (me & reach) > 0
        low, high = jnp.where(upper, other, values), jnp.where(upper, values, other)
        values = jnp.concatenate([low, high])
        reach *= 2
    return values


def exchange(parts):
    return lax.all_to_all(parts, AXES, split_axis=0, concat_axis=0, tiled=True)


def shards(
    density_tiles,
    send_list,
    basis_values,
    active_blocks,
    touch_slots,
    point_weights,
    harmonics,
    shell_index,
    batch_atom,
    radial_green,
):
    devices = lax.axis_size(AXES)
    cols_count = lax.axis_size("col")
    capacity = send_list.shape[2]
    tiles_dev, blk, _ = density_tiles.shape
    batches, points, span = basis_values.shape
    harm_count = harmonics.shape[1]
    radial = radial_green.shape[1]
    slot_count = devices * capacity
    natoms = ATOM_COL * cols_count
    held = -(-harm_count // devices)
    rows = -(-harm_count // 16) * 16

    tile_ids = jnp.transpose(send_list, (2, 0, 1))
    outgoing = gather_tiles(tile_ids, density_tiles)
    outgoing, own_atoms = lax.optimization_barrier((outgoing, batch_atom))
    arrived = exchange(outgoing.reshape(devices, capacity, blk, blk))
    all_atoms = gathered(own_atoms, devices).reshape(devices, batches)
    atom_rows = jnp.broadcast_to(all_atoms.T[:, :, None], (batches, devices, radial))
    received = arrived.reshape(slot_count, blk, blk)

    basis_t = jnp.transpose(basis_values, (0, 2, 1))
    harm_rows = jnp.pad(harmonics, ((0, 2 * batches), (0, rows - harm_count), (0, 0)))
    weights = point_weights[:, None, :]
    shells = shell_index[:, None, :]
    plan = jnp.concatenate(
        [touch_slots.reshape(batches, -1), active_blocks[:, None]], axis=1
    )

    rho, mom_out = density_pass(
        plan, received, basis_t, harm_rows, weights, shells,
        (held, radial), devices,
    )
    mom_in = exchange(mom_out)
    first = lax.axis_index(AXES) * held
    degree_ids = degrees(jnp.minimum(first + jnp.arange(held), harm_count - 1))
    green_own = jnp.concatenate(
        [lax.dynamic_slice_in_dim(radial_green, degree_ids[k], 1) for k in range(held)]
    )
    poles_out = radial_solve(
        mom_in, green_own, atom_rows, natoms, held, batches, cols_count
    )
    poles = exchange(poles_out)
    returning = potential_pass(
        plan, poles, rho, basis_t, harm_rows, weights, shells,
        slot_count, blk, held,
    )
    back = exchange(returning.reshape(devices, capacity, blk, blk))
    ham_tiles = sum_tiles(tile_ids, back.reshape(slot_count, blk, blk), tiles_dev)

    own = poles[:, batches * held :, :].reshape(devices, ATOM_COL, held, radial)
    own = jnp.transpose(own, (1, 0, 2, 3)).reshape(ATOM_COL, devices * held, radial)
    return (ham_tiles, own[:, :harm_count])


def solution(mesh):
    in_specs = (
        P(AXES, None, None),
        P(AXES, None, None),
        P(AXES, None, None),
        P(AXES),
        P(AXES, None, None),
        P(AXES, None),
        P(AXES, None, None),
        P(AXES, None),
        P(AXES),
        P(),
    )
    out_specs = (P(AXES, None, None), P("col", None, None))
    return jax.shard_map(shards, mesh=mesh, in_specs=in_specs, out_specs=out_specs, check_vma=False)
```
